32 devices in a mesh: dp: 16 (over z, y, core), seq: 2 (over x).
Axes of the slice: x: 2, y: 2, z: 4, core: 2. Of those that a mesh axis runs over, the one named last changes fastest.
Arguments:
- tokens: bfloat16 [32, 320, 1024], P('dp', 'seq'), may hold values from -6 to 6
- keep: int32 [32, 320], P('dp', 'seq'), may hold values from 0 to 1, as said below
- norm_gain: bfloat16 [2, 2, 1024], P(None, None, ('dp', 'seq')), may hold values from 0.5 to 1.5
- norm_bias: bfloat16 [2, 2, 1024], P(None, None, ('dp', 'seq')), may hold values from -2 to 2
- qkv_weight: bfloat16 [2, 1024, 3072], P(None, ('dp', 'seq')), may hold values from -0.1875 to 0.1875
- qv_bias: bfloat16 [2, 2, 1024], P(None, None, ('dp', 'seq')), may hold values from -2 to 2
- out_weight: bfloat16 [2, 1024, 1024], P(None, ('dp', 'seq')), may hold values from -0.75 to 0.75
- out_bias: bfloat16 [2, 1024], P(None, ('dp', 'seq')), may hold values from -2 to 2
- up_weight: bfloat16 [2, 1024, 4096], P(None, ('dp', 'seq')), may hold values from -0.1875 to 0.1875
- up_bias: bfloat16 [2, 4096], P(None, ('dp', 'seq')), may hold values from -2 to 2
- down_weight: bfloat16 [2, 4096, 1024], P(None, ('dp', 'seq')), may hold values from -0.09375 to 0.09375
- down_bias: bfloat16 [2, 1024], P(None, ('dp', 'seq')), may hold values from -2 to 2
- cotangent: bfloat16 [32, 320, 1024], P('dp', 'seq'), may hold values from -6 to 6
Outputs:
- output: bfloat16 [32, 320, 1024], P('dp', 'seq')
- input_grad: float32 [32, 320, 1024], P('dp', 'seq')
- grad_norm_gain: float32 [2, 2, 1024], P(None, None, ('dp', 'seq'))
- grad_norm_bias: float32 [2, 2, 1024], P(None, None, ('dp', 'seq'))
- grad_qkv_weight: float32 [2, 1024, 3072], P(None, ('dp', 'seq'))
- grad_qv_bias: float32 [2, 2, 1024], P(None, None, ('dp', 'seq'))
- grad_out_weight: float32 [2, 1024, 1024], P(None, ('dp', 'seq'))
- grad_out_bias: float32 [2, 1024], P(None, ('dp', 'seq'))
- grad_up_weight: float32 [2, 1024, 4096], P(None, ('dp', 'seq'))
- grad_up_bias: float32 [2, 4096], P(None, ('dp', 'seq'))
- grad_down_weight: float32 [2, 4096, 1024], P(None, ('dp', 'seq'))
- grad_down_bias: float32 [2, 1024], P(None, ('dp', 'seq'))
The draws below stay inside these ranges and needn't reach their ends.
Inputs may be any that keep to these rules, and one draw needn't show every extreme that they name: `keep`: 1 marks a kept token; the first 64 tokens of every image take part whatever their entry; each image has its own rate of kept patches.
All inputs are finite; a program needn't handle non-finite values.
Results may differ from the reference program's by a relative error of at most 0.014.
Values may be sent and summed in bfloat16 or wider, within the bound.
No kernel may reach another device: no remote copies, remote signals or barrier semaphores. Data moves between devices by JAX's collectives and lax.ppermute only.
A program may use at most 384 MiB of HBM per device.

```python
import math
import jax
import jax.numpy as jnp
from jax import lax

D = 1024
FF = 4096
HEAD = 64
BUFFER = 64
LAYERS = 2
SEQ = 320
IMAGES = 32


def draw_keep(key, part):
    rate_key, cell_key = jax.random.split(jax.random.fold_in(key, 11))
    rates = jax.random.randint(rate_key, (IMAGES, 1), 10, 61)
    cells = jax.random.randint(cell_key, (IMAGES, SEQ), 0, 100)
    return (cells < rates).astype(jnp.int32)


def strengthened(array, own_key, source, target, blocks, factor):
    def block_of(position):
        return (jnp.arange(array.shape[position]) // (array.shape[position] // blocks)).reshape((-1,) + (1,) * (array.ndim - 1 - position))

    first = jax.random.permutation(own_key, blocks)[block_of(target)]
    far = (block_of(target) + blocks // 2) % blocks
    return jnp.where((block_of(source) == first) | (block_of(source) == far), factor * array, array)


def level_of(own_key, extent, cuts, least, top_value):
    factor_of = 1.0
    for axis_at, shards_of in cuts:
        draws = jax.random.uniform(jax.random.fold_in(jax.random.fold_in(own_key, 6), axis_at), (shards_of,), jnp.float32, least / len(cuts), top_value / len(cuts))
        factor_of = factor_of * jnp.repeat(jnp.exp(draws), extent[axis_at] // shards_of).reshape((-1,) + (1,) * (len(extent) - 1 - axis_at))
    return factor_of


def noise(stream_key, extent, width, reach, pieces=(), kind=jnp.bfloat16):
    values = width * jax.random.normal(stream_key, extent, jnp.float32)
    if pieces:
        values = values * level_of(stream_key, extent, pieces, -0.22, 0.18)
    return jnp.clip(values, -reach, reach).astype(kind)


def bell_draw_with(rng, dims, deviation, bound, cuts, heavy, kind=jnp.bfloat16):
    drawn = deviation * jax.random.normal(rng, dims, jnp.float32)
    if cuts:
        drawn = drawn * level_of(rng, dims, cuts, -0.22, 0.18)
    return jnp.clip(strengthened(drawn, jax.random.fold_in(rng, 3), *heavy), -bound, bound).astype(kind)


def setup_inputs(seed: int = 0) -> dict:
    arg_keys = jax.random.split(jax.random.key(seed), 14)
    tokens = noise(arg_keys[0], (IMAGES, SEQ, D), 1.0, 6.0, ((0, 16), (1, 2)))
    keep = draw_keep(jax.random.fold_in(arg_keys[13], 71), 0)
    norm_gain = jnp.clip(1.0 + 0.1 * jax.random.normal(arg_keys[2], (LAYERS, 2, D), jnp.float32), 0.5, 1.5).astype(jnp.bfloat16)
    norm_bias = noise(arg_keys[3], (LAYERS, 2, D), 0.3, 2.0, ((2, 32),))
    qkv_weight = noise(arg_keys[4], (LAYERS, D, 3 * D), D ** -0.5, 0.1875, ((1, 32),))
    qv_bias = noise(arg_keys[5], (LAYERS, 2, D), 0.3, 2.0, ((2, 32),))
    out_weight = noise(arg_keys[6], (LAYERS, D, D), (D // 16) ** -0.5, 0.75, ((1, 32),))
    out_bias = noise(arg_keys[7], (LAYERS, D), 0.3, 2.0, ((1, 32),))
    up_weight = noise(arg_keys[8], (LAYERS, D, FF), D ** -0.5, 0.1875, ((1, 32),))
    up_bias = noise(arg_keys[9], (LAYERS, FF), 0.3, 2.0, ((1, 32),))
    down_weight = noise(arg_keys[10], (LAYERS, FF, D), FF ** -0.5, 0.09375, ((1, 32),))
    down_bias = noise(arg_keys[11], (LAYERS, D), 0.3, 2.0, ((1, 32),))
    cotangent = bell_draw_with(arg_keys[12], (IMAGES, SEQ, D), 1.0, 6.0, ((0, 16), (1, 2)), (0, 2, 16, 2.0))
    return {"tokens": tokens, "keep": keep, "norm_gain": norm_gain, "norm_bias": norm_bias, "qkv_weight": qkv_weight, "qv_bias": qv_bias, "out_weight": out_weight, "out_bias": out_bias, "up_weight": up_weight, "up_bias": up_bias, "down_weight": down_weight, "down_bias": down_bias, "cotangent": cotangent}


@jax.custom_vjp
def low(v):
    return lax.optimization_barrier(v.astype(jnp.bfloat16)).astype(jnp.float32)

@jax.custom_vjp
def low_back(v):
    return v

def low_keep(v):
    return (low(v), None)

def low_pass(kept, grad):
    return (grad,)

def back_keep(v):
    return (v, None)

def back_low(kept, grad):
    return (low(grad),)
low.defvjp(low_keep, low_pass)
low_back.defvjp(back_keep, back_low)

def norm_rows(x, gain_vec, shift_vec):
    row_mean = lax.optimization_barrier(jnp.mean(x, axis=-1, keepdims=True))
    centered = x - row_mean
    variance = lax.optimization_barrier(jnp.mean(centered * centered, axis=-1, keepdims=True))
    return centered * lax.rsqrt(variance + 1e-06) * gain_vec + shift_vec

def one_layer(x, key_flags, params):
    highest = lax.Precision.HIGHEST
    norm_gain, norm_bias, qkv_weight, qv_bias, out_weight, out_bias, up_weight, up_bias, down_weight, down_bias = params
    n_images, seq_len, model_dim = x.shape
    n_heads = model_dim // HEAD
    normed = low(norm_rows(x, norm_gain[0], norm_bias[0]))
    qkv_all = jnp.einsum('nsd,de->nse', normed, qkv_weight, precision=highest)
    query_f = low(low_back(qkv_all[..., :model_dim] + qv_bias[0]))
    key_f = low(low_back(qkv_all[..., model_dim:2 * model_dim]))
    value_f = low(low_back(qkv_all[..., 2 * model_dim:] + qv_bias[1]))
    shape4 = (n_images, seq_len, n_heads, HEAD)
    scores = jnp.einsum('nqhd,nkhd->nhqk', query_f.reshape(shape4), key_f.reshape(shape4), precision=highest)
    scores = low_back(scores * HEAD ** (-0.5))
    scores = jnp.where(key_flags[:, None, None, :], scores, -1e+30)
    attn_probs = low(jax.nn.softmax(scores, axis=-1))
    attended = jnp.einsum('nhqk,nkhd->nqhd', attn_probs, value_f.reshape(shape4), precision=highest)
    attended = low(low_back(attended.reshape(n_images, seq_len, model_dim)))
    resid_mid = x + low_back(jnp.einsum('nsc,cd->nsd', attended, out_weight, precision=highest)) + out_bias
    normed_two = low(norm_rows(resid_mid, norm_gain[1], norm_bias[1]))
    up_pre = low_back(jnp.einsum('nsd,df->nsf', normed_two, up_weight, precision=highest)) + up_bias
    hidden = low(jax.nn.gelu(up_pre, approximate=False))
    return resid_mid + low_back(jnp.einsum('nsf,fd->nsd', hidden, down_weight, precision=highest)) + down_bias

def encoder(x, key_flags, params):
    for layer_number in range(LAYERS):
        x = one_layer(x, key_flags, tuple((p[layer_number] for p in params)))
    return x * key_flags[..., None].astype(jnp.float32)

def reference(tokens, keep, norm_gain, norm_bias, qkv_weight, qv_bias, out_weight, out_bias, up_weight, up_bias, down_weight, down_bias, cotangent):
    params = tuple((p.astype(jnp.float32) for p in (norm_gain, norm_bias, qkv_weight, qv_bias, out_weight, out_bias, up_weight, up_bias, down_weight, down_bias)))
    positions = jnp.arange(SEQ, dtype=jnp.int32)
    key_flags = (keep == 1) | (positions < BUFFER)[None, :]
    group_size = math.gcd(IMAGES, 8)
    blocks = IMAGES // group_size
    inputs = tokens.astype(jnp.float32).reshape(blocks, group_size, SEQ, D)
    flag_blocks = key_flags.reshape(blocks, group_size, SEQ)
    cot_blocks = cotangent.astype(jnp.float32).reshape(blocks, group_size, SEQ, D)

    def scan_step(grad_acc, batch_item):
        x, flag_rows, cot_rows = batch_item

        def forward(x_in, weights_in):
            return encoder(x_in, flag_rows, weights_in)
        result, pullback = jax.vjp(forward, x, params)
        x_grad, weight_grads = pullback(cot_rows)
        grad_acc = jax.tree.map(jnp.add, grad_acc, weight_grads)
        return (grad_acc, (result.astype(jnp.bfloat16), x_grad))
    zero_grads = tuple((jnp.zeros_like(p) for p in params))
    grad_sums, (outputs, input_grads) = lax.scan(scan_step, zero_grads, (inputs, flag_blocks, cot_blocks))
    return (outputs.reshape(IMAGES, SEQ, D), input_grads.reshape(IMAGES, SEQ, D), grad_sums[0], grad_sums[1], grad_sums[2], grad_sums[3], grad_sums[4], grad_sums[5], grad_sums[6], grad_sums[7], grad_sums[8], grad_sums[9])
```

```python
import jax
import jax.numpy as jnp
from jax import lax
from jax.experimental import pallas as pl
from jax.experimental.pallas import tpu as pltpu
from jax.sharding import PartitionSpec as P

HEAD = 64
BUFFER = 64
LAYERS = 2
AXES = ("dp", "seq")

masked_score = -1e30
f32 = jnp.float32
bf16 = jnp.bfloat16


def norm_rows(x, gain_vec, shift_vec):
    row_mean = jnp.mean(x, axis=-1, keepdims=True)
    centered = x - row_mean
    variance = jnp.mean(centered * centered, axis=-1, keepdims=True)
    return centered * lax.rsqrt(variance + 1e-06) * gain_vec + shift_vec


def gelu_exact(v):
    return jax.nn.gelu(v, approximate=False)


def exchange(value, mask, n):
    return lax.ppermute(value, AXES, [(i, i ^ mask) for i in range(n)])


def mask_orders(n):
    bits = n.bit_length() - 1
    across, partner = 1, 2
    near = [4] if bits > 2 else []
    far = [(1 << k) | (1 << (k - 1)) if k > 3 else 1 << k for k in range(bits - 1, 2, -1)]
    return {
        "up": far + [across] + near + [partner],
        "down": far + near + [across] + [partner],
        "qkv": [across] + near + far + [partner],
    }


def span_table(masks):
    table = [0]
    for m in masks:
        table = table + [t ^ m for t in table]
    return table


def positions_of(masks, me):
    n = 1 << len(masks)
    table = span_table(masks)
    inverse = [0] * n
    for p, t in enumerate(table):
        inverse[t] = p
    inverse = jnp.asarray(inverse, jnp.int32)
    return inverse[me ^ jnp.arange(n, dtype=jnp.int32)]


def owners_of(masks, me):
    return me ^ jnp.asarray(span_table(masks), jnp.int32)


def reorder_body(order, src, dst):
    dst[...] = src[...]


def reorder(blocks, order):
    n, rows, cols = blocks.shape
    spec_in = pl.BlockSpec((1, rows, cols), lambda j, o: (o[j], 0, 0))
    spec_out = pl.BlockSpec((1, rows, cols), lambda j, o: (j, 0, 0))
    size = blocks.size * blocks.dtype.itemsize
    return pl.pallas_call(
        reorder_body,
        grid_spec=pltpu.PrefetchScalarGridSpec(
            num_scalar_prefetch=1, grid=(n,), in_specs=[spec_in], out_specs=spec_out
        ),
        out_shape=jax.ShapeDtypeStruct(blocks.shape, blocks.dtype),
        cost_estimate=pl.CostEstimate(flops=0, bytes_accessed=2 * size, transcendentals=0),
        name="reorder",
    )(order, blocks)


def gather(own, masks, me, n):
    held = own[None]
    for m in masks:
        held = jnp.concatenate([held, exchange(held, m, n)], axis=0)
    whole = reorder(held, positions_of(masks, me))
    return whole.reshape(n * own.shape[0], own.shape[1])


def scatter_sum(whole, masks, me, n):
    rows, cols = whole.shape
    held = reorder(whole.reshape(n, rows // n, cols), owners_of(masks, me))
    for m in reversed(masks):
        half = held.shape[0] // 2
        got = exchange(held[half:], m, n)
        total = held[:half].astype(f32) + got.astype(f32)
        held = total if half == 1 else total.astype(bf16)
    return held[0]


def attention_scores(query_h, key_h, key_flags, attention_score_scale):
    scores = (
        jnp.einsum("qhd,khd->hqk", query_h, key_h, preferred_element_type=f32)
        * attention_score_scale
    )
    return jnp.where(key_flags[None, None, :] > 0, scores, masked_score)


def layer_forward(x_rows, key_flags, vectors, w_qkv, w_up_out, w_down, scale):
    length, model_dim = x_rows.shape
    n_heads = model_dim // HEAD
    hidden_dim = w_down.shape[0]
    gains, shifts, qv_shift, out_shift, up_shift, down_shift = vectors
    normed = norm_rows(x_rows, gains[0], shifts[0]).astype(bf16)
    qkv_all = jnp.dot(normed, w_qkv, preferred_element_type=f32)
    query_bf = (qkv_all[:, :model_dim] + qv_shift[0]).astype(bf16)
    key_bf = qkv_all[:, model_dim : 2 * model_dim].astype(bf16)
    value_bf = (qkv_all[:, 2 * model_dim : 3 * model_dim] + qv_shift[1]).astype(bf16)
    query_h = query_bf.reshape(length, n_heads, HEAD)
    key_h = key_bf.reshape(length, n_heads, HEAD)
    value_h = value_bf.reshape(length, n_heads, HEAD)
    scores = attention_scores(query_h, key_h, key_flags, scale)
    row_max = jnp.max(scores, axis=-1, keepdims=True)
    row_sum = jnp.sum(jnp.exp(scores - row_max), axis=-1, keepdims=True)
    log_total = row_max + jnp.log(row_sum)
    attn_probs = jnp.exp(scores - log_total).astype(bf16)
    attended = jnp.einsum("hqk,khd->qhd", attn_probs, value_h, preferred_element_type=f32)
    attended = attended.reshape(length, model_dim).astype(bf16)
    w_out = w_up_out[:, hidden_dim:]
    resid_mid = x_rows + jnp.dot(attended, w_out, preferred_element_type=f32) + out_shift
    normed_two = norm_rows(resid_mid, gains[1], shifts[1]).astype(bf16)
    w_up = w_up_out[:, :hidden_dim]
    up_pre = jnp.dot(normed_two, w_up, preferred_element_type=f32) + up_shift
    hidden = gelu_exact(up_pre).astype(bf16)
    result = resid_mid + jnp.dot(hidden, w_down, preferred_element_type=f32) + down_shift
    saved = (
        x_rows,
        normed,
        query_h,
        key_h,
        value_h,
        key_flags,
        log_total,
        attended,
        resid_mid,
        normed_two,
        up_pre,
        hidden,
    )
    return result, saved


def layer_backward(grad_rows, saved, vectors, w_qkv, w_up_out, w_down, scale):
    (
        x_rows,
        normed,
        query_h,
        key_h,
        value_h,
        key_flags,
        log_total,
        attended,
        resid_mid,
        normed_two,
        up_pre,
        hidden,
    ) = saved
    gains, shifts, qv_shift, out_shift, up_shift, down_shift = vectors
    length, model_dim = x_rows.shape
    hidden_dim = w_down.shape[0]
    grad_bf = grad_rows.astype(bf16)
    g_down = jnp.einsum("rf,rd->fd", hidden, grad_bf, preferred_element_type=f32).astype(bf16)
    g_down_shift = jnp.sum(grad_rows, axis=0)
    d_hidden = jnp.einsum("rd,fd->rf", grad_bf, w_down, preferred_element_type=f32)
    d_up = jax.vjp(gelu_exact, up_pre)[1](d_hidden)[0]
    d_up_bf = d_up.astype(bf16)
    g_up = jnp.einsum("rd,rf->df", normed_two, d_up_bf, preferred_element_type=f32).astype(bf16)
    g_up_shift = jnp.sum(d_up, axis=0)
    w_up = w_up_out[:, :hidden_dim]
    d_normed_two = jnp.einsum("rf,df->rd", d_up_bf, w_up, preferred_element_type=f32)
    norm_back_two = jax.vjp(norm_rows, resid_mid, gains[1], shifts[1])[1]
    d_mid, g_gain_two, g_shift_two = norm_back_two(d_normed_two)
    d_mid = grad_rows + d_mid
    d_mid_bf = d_mid.astype(bf16)
    g_out = jnp.einsum("rc,rd->cd", attended, d_mid_bf, preferred_element_type=f32).astype(bf16)
    g_out_shift = jnp.sum(d_mid, axis=0)
    w_out = w_up_out[:, hidden_dim:]
    d_attended = jnp.einsum("rd,cd->rc", d_mid_bf, w_out, preferred_element_type=f32)
    d_attended = d_attended.astype(bf16).reshape(query_h.shape)
    scores = attention_scores(query_h, key_h, key_flags, scale)
    attn_probs = jnp.exp(scores - log_total)
    probs_bf = attn_probs.astype(bf16)
    d_value = jnp.einsum("hqk,qhd->khd", probs_bf, d_attended, preferred_element_type=f32)
    d_probs = jnp.einsum("qhd,khd->hqk", d_attended, value_h, preferred_element_type=f32)
    inner = jnp.sum(attn_probs * d_probs, axis=-1, keepdims=True)
    d_scores = (attn_probs * (d_probs - inner)).astype(bf16)
    d_query = jnp.einsum("hqk,khd->qhd", d_scores, key_h, preferred_element_type=f32) * scale
    d_key = jnp.einsum("hqk,qhd->khd", d_scores, query_h, preferred_element_type=f32) * scale
    d_query_bf = d_query.reshape(length, model_dim).astype(bf16)
    d_key_bf = d_key.reshape(length, model_dim).astype(bf16)
    d_value_bf = d_value.reshape(length, model_dim).astype(bf16)
    d_qkv = jnp.concatenate([d_query_bf, d_key_bf, d_value_bf], axis=1)
    g_qkv = jnp.einsum("rd,re->de", normed, d_qkv, preferred_element_type=f32).astype(bf16)
    g_query_shift = jnp.sum(d_query_bf.astype(f32), axis=0)
    g_value_shift = jnp.sum(d_value_bf.astype(f32), axis=0)
    d_normed = jnp.einsum("re,de->rd", d_qkv, w_qkv, preferred_element_type=f32)
    norm_back_one = jax.vjp(norm_rows, x_rows, gains[0], shifts[0])[1]
    d_rows, g_gain_one, g_shift_one = norm_back_one(d_normed)
    d_rows = d_mid + d_rows
    vector_grads = [
        g_gain_one,
        g_gain_two,
        g_shift_one,
        g_shift_two,
        g_query_shift,
        g_value_shift,
        g_out_shift,
        g_down_shift,
        g_up_shift,
    ]
    return d_rows, vector_grads, g_qkv, jnp.concatenate([g_up, g_out], axis=1), g_down


def per_device(
    n_devices,
    tokens,
    keep,
    norm_gain,
    norm_bias,
    qkv_weight,
    qv_bias,
    out_weight,
    out_bias,
    up_weight,
    up_bias,
    down_weight,
    down_bias,
    cotangent,
):
    n = n_devices
    seq_at = lax.axis_index("seq")
    me = lax.axis_index("dp") * 2 + seq_at
    n_images, local_len, model_dim = tokens.shape
    half_images = n_images // 2
    scale = HEAD ** (-0.5)
    orders = mask_orders(n)
    width = norm_gain.shape[2]
    ratio = up_bias.shape[1] // width

    positions = seq_at * local_len + lax.iota(jnp.int32, local_len)
    key_keep = ((keep == 1) | (positions < BUFFER)[None, :]).astype(bf16)

    def halves(value):
        low, high = value[:half_images], value[half_images:]
        mine = jnp.where(seq_at == 0, low, high)
        other = jnp.where(seq_at == 0, high, low)
        return mine, other

    def joined(mine, other):
        return jnp.where(
            seq_at == 0,
            jnp.concatenate([mine, other], axis=0),
            jnp.concatenate([other, mine], axis=0),
        )

    keep_mine, keep_other = halves(key_keep)
    tok_mine, tok_other = halves(tokens)
    cot_mine, cot_other = halves(cotangent)
    keep_all = jnp.concatenate([keep_mine, exchange(keep_other, 1, n)], axis=1)
    tok_all = jnp.concatenate([tok_mine, exchange(tok_other, 1, n)], axis=1)
    cot_all = jnp.concatenate([cot_mine, exchange(cot_other, 1, n)], axis=1)

    def columns(l):
        return [norm_gain[l, 0], norm_gain[l, 1], norm_bias[l, 0], norm_bias[l, 1]] + [
            qv_bias[l, 0],
            qv_bias[l, 1],
            out_bias[l],
            down_bias[l],
        ] + [up_bias[l, q * width : (q + 1) * width] for q in range(ratio)]

    stacked = jnp.stack(sum([columns(l) for l in range(LAYERS)], []))
    per_layer = stacked.shape[0] // LAYERS
    side = 128
    stacked = jnp.pad(stacked, ((0, side - stacked.shape[0]), (0, 0))).T

    w_qkv, w_up_out, w_down = [], [], []
    for l in range(LAYERS):
        own = qkv_weight[l]
        if l == 0:
            own = jnp.concatenate([own, stacked], axis=1)
        w_qkv.append(gather(own, orders["qkv"], me, n))
        own = jnp.concatenate([up_weight[l], out_weight[l]], axis=1)
        w_up_out.append(gather(own, orders["up"], me, n))
        w_down.append(gather(down_weight[l], orders["down"], me, n))
    table = w_qkv[0][:, 3 * model_dim :].T.astype(f32)
    w_qkv[0] = w_qkv[0][:, : 3 * model_dim]

    vectors = []
    for l in range(LAYERS):
        rows = table[l * per_layer : (l + 1) * per_layer]
        up_shift = rows[8:].reshape(ratio, n, width).transpose(1, 0, 2).reshape(-1)
        vectors.append((rows[0:2], rows[2:4], rows[4:6], rows[6], up_shift, rows[7]))
    vectors = [(g, s, qv, o, u, d) for g, s, qv, o, u, d in vectors]

    outputs, input_grads = [], []
    sums = None
    for image in range(half_images):
        x = tok_all[image].astype(f32)
        flags = keep_all[image]
        saves = []
        for l in range(LAYERS):
            x, saved = layer_forward(x, flags, vectors[l], w_qkv[l], w_up_out[l], w_down[l], scale)
            saves.append(saved)
        mask_rows = flags.astype(f32)[:, None]
        outputs.append((x * mask_rows).astype(bf16))
        grad = cot_all[image].astype(f32) * mask_rows
        parts = [None] * LAYERS
        for l in reversed(range(LAYERS)):
            grad, vg, g_qkv, g_up_out, g_down = layer_backward(
                grad, saves[l], vectors[l], w_qkv[l], w_up_out[l], w_down[l], scale
            )
            parts[l] = (vg, g_qkv, g_up_out, g_down)
        input_grads.append(grad.astype(bf16))
        sums = parts if sums is None else jax.tree.map(jnp.add, sums, parts)

    out_qkv, out_up, out_out, out_down = [None] * 2, [None] * 2, [None] * 2, [None] * 2
    hidden_dim = up_bias.shape[1] * n
    vector_out = None
    for l in reversed(range(LAYERS)):
        vg, g_qkv, g_up_out, g_down = sums[l]
        out_down[l] = scatter_sum(g_down, orders["down"], me, n)
        both = scatter_sum(g_up_out, orders["up"], me, n)
        out_up[l], out_out[l] = both[:, :hidden_dim], both[:, hidden_dim:]
        if l == 0:
            rows = []
            for k in range(LAYERS):
                vk = sums[k][0]
                rows += vk[:8]
                up_rows = vk[8].reshape(n, ratio, width).transpose(1, 0, 2).reshape(ratio, -1)
                rows += [up_rows[q] for q in range(ratio)]
            rows = jnp.stack(rows)
            rows = jnp.pad(rows, ((0, side - rows.shape[0]), (0, 0))).T.astype(bf16)
            g_qkv = jnp.concatenate([g_qkv, rows], axis=1)
        got = scatter_sum(g_qkv, orders["qkv"], me, n)
        out_qkv[l] = got[:, : 3 * model_dim]
        if l == 0:
            vector_out = got[:, 3 * model_dim :].T

    def pick(at):
        return jnp.stack([vector_out[l * per_layer + at] for l in range(LAYERS)])

    grad_gain = jnp.stack([pick(0), pick(1)], axis=1)
    grad_shift = jnp.stack([pick(2), pick(3)], axis=1)
    grad_qv = jnp.stack([pick(4), pick(5)], axis=1)
    grad_up_shift = jnp.concatenate([pick(8 + q) for q in range(ratio)], axis=1)

    def handed_back(values):
        whole = jnp.stack(values)
        back = exchange(whole[:, local_len:], 1, n)
        return joined(whole[:, :local_len], back)

    return (
        handed_back(outputs),
        handed_back(input_grads).astype(f32),
        grad_gain,
        grad_shift,
        jnp.stack(out_qkv),
        grad_qv,
        jnp.stack(out_out),
        pick(6),
        jnp.stack(out_up),
        grad_up_shift,
        jnp.stack(out_down),
        pick(7),
    )


def solution(mesh):
    n_devices = mesh.shape["dp"] * mesh.shape["seq"]
    rows = P(None, AXES, None)
    last = P(None, None, AXES)
    flat = P(None, AXES)
    batch = P("dp", "seq", None)

    def body(*args):
        return per_device(n_devices, *args)

    return jax.shard_map(
        body,
        mesh=mesh,
        in_specs=(
            batch,
            P("dp", "seq"),
            last,
            last,
            rows,
            last,
            rows,
            flat,
            rows,
            flat,
            rows,
            flat,
            batch,
        ),
        out_specs=(batch, batch, last, last, rows, last, rows, flat, rows, flat, rows, flat),
        check_vma=False,
    )
```

```python
import functools

import jax
import jax.numpy as jnp
from jax import lax
from jax.experimental import pallas as pl
from jax.experimental.pallas import tpu as pltpu
from jax.sharding import PartitionSpec as P

HEAD = 64
BUFFER = 64
LAYERS = 2
AXES = ("dp", "seq")
BLOCKS = 32
SIDE = 128

masked_score = -1e30
f32 = jnp.float32
bf16 = jnp.bfloat16
INV_SQRT2 = 0.7071067811865476
INV_SQRT2PI = 0.3989422804014327

VMEM = pl.BlockSpec(memory_space=pltpu.VMEM)
SMEM = pl.BlockSpec(memory_space=pltpu.SMEM)
ANY = pl.BlockSpec(memory_space=pl.ANY)
weight_now = [10]
VMEM_LIMIT = 58 * 1024 * 1024


def mm(a, b):
    return lax.dot_general(a, b, (((1,), (0,)), ((), ())), preferred_element_type=f32)


def mm_nt(a, b):
    return lax.dot_general(a, b, (((1,), (1,)), ((), ())), preferred_element_type=f32)


def mm_tn(a, b):
    return lax.dot_general(a, b, (((0,), (0,)), ((), ())), preferred_element_type=f32)


def centred(x):
    mean = jnp.mean(x, axis=-1, keepdims=True)
    c = x - mean
    r = lax.rsqrt(jnp.mean(c * c, axis=-1, keepdims=True) + 1e-06)
    return c * r, r


def norm_back(d, n, r, gain):
    e = d * gain
    mean_e = jnp.mean(e, axis=-1, keepdims=True)
    mean_en = jnp.mean(e * n, axis=-1, keepdims=True)
    return r * (e - mean_e - n * mean_en)


def columns_sum(v):
    return jnp.sum(v, axis=0, keepdims=True)


def fetch(colors, parts, me, dst, sem, start=0):
    stop = start + dst.shape[1]
    for first, width, table, at, per, base, fixed in colors:
        low, high = max(start, first), min(stop, first + width)
        if low >= high:
            continue
        rows = dst.shape[0] // len(table)
        for p, offset in enumerate(table):
            owner = p if fixed else me ^ offset
            to_rows = pl.ds(pl.multiple_of(owner * rows, rows), rows)
            cols = pl.ds(low - first, high - low)
            src = parts[at + p // per].at[p % per, pl.ds(base, rows), cols]
            to = dst.at[to_rows, pl.ds(low - start, high - low)]
            pltpu.make_async_copy(src, to, sem).start()


def arrived(dst, sem):
    pltpu.make_async_copy(dst, dst, sem).wait()


def spread(src, out, me, arrays, sem, start):
    first, _, table, at, per, base, fixed = out
    width = src.shape[1]
    rows = src.shape[0] // len(table)
    for p, offset in enumerate(table):
        owner = p if fixed else me ^ offset
        from_rows = pl.ds(pl.multiple_of(owner * rows, rows), rows)
        to = arrays[at + p // per].at[p % per, pl.ds(base, rows), pl.ds(start, width)]
        pltpu.make_async_copy(src.at[from_rows, :], to, sem).start()


def holds(outs, column):
    return [o for o in outs if o[0] <= column < o[0] + o[1]][0]


def attn_fwd_body(colors, many, me_ref, x_ref, flag_ref, gain_ref, shift_ref, bias_ref, *refs):
    parts, refs = refs[:many], refs[many:]
    normed_ref, qkv_ref, att_ref, lse_ref, w, sem = refs
    dim = x_ref.shape[1]
    fetch(colors, parts, me_ref[0], w, sem)
    n, _ = centred(x_ref[...].astype(f32))
    normed_ref[...] = (n * gain_ref[...] + shift_ref[...]).astype(bf16)
    arrived(w, sem)

    def project(c, carry):
        cols = pl.ds(pl.multiple_of(c * 512, 512), 512)
        qkv_ref[:, cols] = (mm(normed_ref[...], w[:, cols]) + bias_ref[:, cols]).astype(bf16)
        return carry

    lax.fori_loop(0, 3 * dim // 512, project, 0)
    allowed = flag_ref[...] > 0
    scale = HEAD ** (-0.5)

    def two_heads(hp, carry):
        base = pl.multiple_of(hp * 128, 128)
        q2 = qkv_ref[:, pl.ds(base, 128)]
        k2 = qkv_ref[:, pl.ds(pl.multiple_of(dim + hp * 128, 128), 128)]
        v2 = qkv_ref[:, pl.ds(pl.multiple_of(2 * dim + hp * 128, 128), 128)]
        outs = []
        for s in range(2):
            cut = slice(s * HEAD, (s + 1) * HEAD)
            score = jnp.where(allowed, mm_nt(k2[:, cut], q2[:, cut]) * scale, masked_score)
            top = jnp.max(score, axis=0, keepdims=True)
            e = jnp.exp(score - top)
            total = jnp.sum(e, axis=0, keepdims=True)
            probs = (e * (1.0 / total)).astype(bf16)
            lse_ref[pl.ds(2 * hp + s, 1), :] = top + jnp.log(total)
            outs.append(mm_tn(probs, v2[:, cut]))
        att_ref[:, pl.ds(base, 128)] = jnp.concatenate(outs, axis=1).astype(bf16)
        return carry

    lax.fori_loop(0, dim // 128, two_heads, 0)


def mlp_up_body(colors, many, me_ref, x_ref, att_ref, ob_ref, gain_ref, shift_ref, ub_ref, *refs):
    parts, refs = refs[:many], refs[many:]
    mid_ref, normed_ref, hidden_ref, slope_ref, w_out, w_up, sem = refs
    ff = ub_ref.shape[1]
    fetch(colors, parts, me_ref[0], w_out, sem.at[0], ff)
    fetch(colors, parts, me_ref[0], w_up, sem.at[1])
    arrived(w_out, sem.at[0])
    mid = x_ref[...].astype(f32) + mm(att_ref[...], w_out[...]) + ob_ref[...]
    mid_ref[...] = mid
    n, _ = centred(mid)
    normed_ref[...] = (n * gain_ref[...] + shift_ref[...]).astype(bf16)
    arrived(w_up, sem.at[1])

    def step(c, carry):
        cols = pl.ds(pl.multiple_of(c * 512, 512), 512)
        u = mm(normed_ref[...], w_up[:, cols]) + ub_ref[:, cols]
        phi = 0.5 + 0.5 * lax.erf(u * INV_SQRT2)
        hidden_ref[:, cols] = (u * phi).astype(bf16)
        slope_ref[:, cols] = phi + u * (INV_SQRT2PI * jnp.exp(-0.5 * u * u))
        return carry

    lax.fori_loop(0, ff // 512, step, 0)


def mlp_down_body(colors, many, last, me_ref, mid_ref, hidden_ref, db_ref, flag_ref, *refs):
    parts, refs = refs[:many], refs[many:]
    out_ref, w, sem = refs
    fetch(colors, parts, me_ref[0], w, sem)
    arrived(w, sem)
    for c in range(0, w.shape[1], 512):
        cols = slice(c, c + 512)
        y = mid_ref[:, cols] + mm(hidden_ref[...], w[:, cols]) + db_ref[:, cols]
        if last:
            y = (y * flag_ref[...]).astype(bf16)
        out_ref[:, cols] = y


def down_grad_body(outs, many, me_ref, grad_ref, hidden_ref, *refs):
    arrays, refs = refs[:many], refs[many:]
    low_ref, sum_ref, perm, tile, sem = refs
    me = me_ref[0]
    grad = grad_ref[...]
    low_ref[...] = grad.astype(bf16)
    sum_ref[...] = columns_sum(grad)
    group = 4
    ((first, width, table, at, per, base, fixed),) = outs
    rows = hidden_ref.shape[1] // len(table)
    for p, offset in enumerate(table):
        owner = pl.ds(pl.multiple_of((p if fixed else me ^ offset) * rows, rows), rows)
        perm[:, p * rows : (p + 1) * rows] = hidden_ref[:, owner]
    pending = [None, None]
    for g in reversed(range(len(table) // group)):
        slot = g % 2
        if pending[slot] is not None:
            pending[slot].wait()
        cut = slice(g * group * rows, (g + 1) * group * rows)
        block = mm_tn(perm[:, cut], low_ref[...])
        tile[slot] = block.astype(bf16).reshape(tile.shape[1:])
        b0 = g * group
        to = arrays[at + b0 // per].at[pl.ds(b0 % per, group), pl.ds(base, rows)]
        pending[slot] = pltpu.make_async_copy(tile.at[slot], to, sem.at[slot])
        pending[slot].start()
    for copy in pending:
        copy.wait()


def mlp_back_body(ups, downs, outs, many, me_ref, grad_ref, low_ref, slope_ref, mid_ref, *refs):
    normed_ref, att_ref, gain_ref, refs = refs[0], refs[1], refs[2], refs[3:]
    many_up, many_down, many_in, many_out = many
    up_parts, refs = refs[:many_up], refs[many_up:]
    down_parts, refs = refs[:many_down], refs[many_down:]
    refs = refs[many_in:]
    halves, refs = refs[:many_out], refs[many_out:]
    d_mid_ref, d_att_ref, g_up_ref, g_gain, g_shift, g_out, refs = (*refs[:6], refs[6:])
    w_down, w_up, w_out, turned, turned_att, d_low_ref, acc, tile, low_mid, sem, out_sem = refs
    me = me_ref[0]
    ff, dim = w_down.shape
    fetch(downs, down_parts, me, w_down, sem.at[0])
    fetch(ups, up_parts, me, w_up, sem.at[1])
    fetch(ups, up_parts, me, w_out, sem.at[2], ff)
    turned[...] = normed_ref[...].T
    turned_att[...] = att_ref[...].T
    acc[...] = jnp.zeros_like(acc)
    arrived(w_down, sem.at[0])

    def first_step(c, carry):
        cols = pl.ds(pl.multiple_of(c * 512, 512), 512)
        d_up = mm_nt(low_ref[...], w_down[cols, :]) * slope_ref[:, cols]
        g_up_ref[:, cols] = columns_sum(d_up)
        d_low_ref[:, cols] = d_up.astype(bf16)
        return carry

    lax.fori_loop(0, ff // 512, first_step, 0)
    arrived(w_up, sem.at[1])

    def flush(slot):
        pltpu.make_async_copy(tile.at[slot], tile.at[slot], out_sem.at[slot]).wait()

    for out in outs:
        first, width = out[:2]
        stop = min(first + width, ff)

        def step(c, carry, out=out, first=first):
            start = pl.multiple_of(c * 512, 512)
            cols = pl.ds(start, 512)
            slot = lax.rem(c, 2)

            @pl.when(c >= 2)
            def _():
                flush(slot)

            tile[slot] = mm(turned[...], d_low_ref[:, cols]).astype(bf16)
            local = pl.multiple_of(start - first, 512)
            spread(tile.at[slot], out, me, halves, out_sem.at[slot], local)
            acc[...] += mm_nt(d_low_ref[:, cols], w_up[:, cols])
            return carry

        lax.fori_loop(first // 512, stop // 512, step, 0)
    n, r = centred(mid_ref[...])
    d = acc[...]
    g_gain[...] = columns_sum(d * n)
    g_shift[...] = columns_sum(d)
    d_mid = grad_ref[...] + norm_back(d, n, r, gain_ref[...])
    d_mid_ref[...] = d_mid
    g_out[...] = columns_sum(d_mid)
    low_mid[...] = d_mid.astype(bf16)
    arrived(w_out, sem.at[2])
    for c in range(dim // 512):
        flush(c % 2)
        tile[c % 2] = mm(turned_att[...], low_mid[:, c * 512 : (c + 1) * 512]).astype(bf16)
        start = ff + c * 512
        out = holds(outs, start)
        spread(tile.at[c % 2], out, me, halves, out_sem.at[c % 2], start - out[0])
    d_att_ref[...] = mm_nt(low_mid[...], w_out[...]).astype(bf16)
    flush(0)
    flush(1)


def attn_back_body(colors, outs, counts, extra, me_ref, d_att_ref, qkv_ref, lse_ref, flag_ref, *refs):
    many, many_in, many_out = counts
    normed_ref, x_ref, d_mid_ref, gain_ref, refs = *refs[:4], refs[4:]
    if extra:
        others_ref, refs = refs[0], refs[1:]
    parts, refs = refs[:many], refs[many:]
    refs = refs[many_in:]
    halves, refs = refs[:many_out], refs[many_out:]
    d_x_ref, g_gain, g_shift, g_query, g_value, refs = (*refs[:5], refs[5:])
    if extra:
        w, d_qkv, turned, tile, sem, out_sem, column, wide = refs
    else:
        w, d_qkv, turned, tile, sem, out_sem = refs
    me = me_ref[0]
    dim = x_ref.shape[1]
    fetch(colors, parts, me, w, sem)
    turned[...] = normed_ref[...].T
    allowed = flag_ref[...] > 0
    scale = HEAD ** (-0.5)

    def two_heads(hp, carry):
        at_q = pl.ds(pl.multiple_of(hp * 128, 128), 128)
        at_k = pl.ds(pl.multiple_of(dim + hp * 128, 128), 128)
        at_v = pl.ds(pl.multiple_of(2 * dim + hp * 128, 128), 128)
        q2, k2, v2, d2 = qkv_ref[:, at_q], qkv_ref[:, at_k], qkv_ref[:, at_v], d_att_ref[:, at_q]
        dq, dk, dv = [], [], []
        for s in range(2):
            cut = slice(s * HEAD, (s + 1) * HEAD)
            q, k, v, d = q2[:, cut], k2[:, cut], v2[:, cut], d2[:, cut]
            score = jnp.where(allowed, mm_nt(k, q) * scale, masked_score)
            probs = jnp.exp(score - lse_ref[pl.ds(2 * hp + s, 1), :])
            dv.append(mm(probs.astype(bf16), d))
            d_probs = mm_nt(v, d)
            inner = jnp.sum(probs * d_probs, axis=0, keepdims=True)
            d_score = (probs * (d_probs - inner)).astype(bf16)
            dq.append(mm_tn(d_score, k) * scale)
            dk.append(mm(d_score, q) * scale)
        d_qkv[:, at_q] = jnp.concatenate(dq, axis=1).astype(bf16)
        d_qkv[:, at_k] = jnp.concatenate(dk, axis=1).astype(bf16)
        d_qkv[:, at_v] = jnp.concatenate(dv, axis=1).astype(bf16)
        return carry

    lax.fori_loop(0, dim // 128, two_heads, 0)

    def flush(slot):
        pltpu.make_async_copy(tile.at[slot], tile.at[slot], out_sem.at[slot]).wait()

    for c in range(3 * dim // 512):
        if c >= 2:
            flush(c % 2)
        tile[c % 2] = mm(turned[...], d_qkv[:, c * 512 : (c + 1) * 512]).astype(bf16)
        out = holds(outs, c * 512)
        spread(tile.at[c % 2], out, me, halves, out_sem.at[c % 2], c * 512 - out[0])
    g_query[...] = columns_sum(d_qkv[:, :dim].astype(f32))
    g_value[...] = columns_sum(d_qkv[:, 2 * dim :].astype(f32))
    arrived(w, sem)
    d = mm_nt(d_qkv[...], w[...])
    n, r = centred(x_ref[...].astype(f32))
    g_gain[...] = columns_sum(d * n)
    g_shift[...] = columns_sum(d)
    d_x_ref[...] = (d_mid_ref[...] + norm_back(d, n, r, gain_ref[...])).astype(d_x_ref.dtype)
    if extra:
        wide[...] = others_ref[...]
        for at, row in zip(extra, (g_gain, g_shift, g_query, g_value)):
            wide[at : at + 1, :] = row[...]
        column[...] = wide[...].T.astype(bf16)
        spread(column, outs[-1], me, halves, sem, 3 * dim - outs[-1][0])
        arrived(column, sem)
    flush(0)
    flush(1)


def shaped(shape, dtype=f32):
    return jax.ShapeDtypeStruct(shape, dtype)


def call(body, name, in_specs, out_shapes, out_specs, scratch, args, aliases=None):
    return pl.pallas_call(
        body,
        in_specs=in_specs,
        out_specs=out_specs,
        out_shape=out_shapes,
        scratch_shapes=scratch,
        input_output_aliases=aliases or {},
        compiler_params=pltpu.CompilerParams(vmem_limit_bytes=VMEM_LIMIT),
        cost_estimate=pl.CostEstimate(
            flops=10 ** weight_now[0], bytes_accessed=0, transcendentals=0
        ),
        name=name,
    )(*args)


def attn_fwd(me, x, flag, gain, shift, bias, weight):
    length, dim = x.shape
    colors, parts = weight
    return call(
        functools.partial(attn_fwd_body, colors, len(parts)),
        "attn_fwd",
        [SMEM] + [VMEM] * 5 + [ANY] * len(parts),
        (
            shaped((length, dim), bf16),
            shaped((length, 3 * dim), bf16),
            shaped((length, dim), bf16),
            shaped((dim // HEAD, length)),
        ),
        (VMEM,) * 4,
        [pltpu.VMEM((dim, 3 * dim), bf16), pltpu.SemaphoreType.DMA],
        (me, x, flag, gain, shift, bias, *parts),
    )


def mlp_up(me, x, att, out_bias, gain, shift, up_bias, weight):
    length, dim = x.shape
    ff = up_bias.shape[1]
    colors, parts = weight
    return call(
        functools.partial(mlp_up_body, colors, len(parts)),
        "mlp_up",
        [SMEM] + [VMEM] * 6 + [ANY] * len(parts),
        (
            shaped((length, dim)),
            shaped((length, dim), bf16),
            shaped((length, ff), bf16),
            shaped((length, ff)),
        ),
        (VMEM,) * 4,
        [
            pltpu.VMEM((dim, dim), bf16),
            pltpu.VMEM((dim, ff), bf16),
            pltpu.SemaphoreType.DMA((2,)),
        ],
        (me, x, att, out_bias, gain, shift, up_bias, *parts),
    )


def mlp_down(me, mid, hidden, down_bias, flag, weight, last):
    length, dim = mid.shape
    ff = hidden.shape[1]
    colors, parts = weight
    return call(
        functools.partial(mlp_down_body, colors, len(parts), last),
        "mlp_down",
        [SMEM] + [VMEM] * 4 + [ANY] * len(parts),
        shaped((length, dim), bf16 if last else f32),
        VMEM,
        [pltpu.VMEM((ff, dim), bf16), pltpu.SemaphoreType.DMA],
        (me, mid, hidden, down_bias, flag, *parts),
    )


def down_grad(me, grad, hidden, outs, shapes):
    length, dim = grad.shape
    ff = hidden.shape[1]
    return call(
        functools.partial(down_grad_body, outs, len(shapes)),
        "down_grad",
        [SMEM, VMEM, VMEM],
        (*shapes, shaped((length, dim), bf16), shaped((1, dim))),
        (ANY,) * len(shapes) + (VMEM, VMEM),
        [
            pltpu.VMEM((length, ff), bf16),
            pltpu.VMEM((2, 4, ff // BLOCKS, dim), bf16),
            pltpu.SemaphoreType.DMA((2,)),
        ],
        (me, grad, hidden),
    )


def mlp_back(me, grad, low, slope, mid, normed, att, gain, up_weight, down_weight, outs, shapes, old):
    length, dim = grad.shape
    ff = slope.shape[1]
    ups, up_parts = up_weight
    downs, down_parts = down_weight
    many = (len(up_parts), len(down_parts), len(old), len(shapes))
    row = shaped((1, dim))
    return call(
        functools.partial(mlp_back_body, ups, downs, outs, many),
        "mlp_back",
        [SMEM] + [VMEM] * 7 + [ANY] * (len(up_parts) + len(down_parts) + len(old)),
        (
            *shapes,
            shaped((length, dim)),
            shaped((length, dim), bf16),
            shaped((1, ff)),
            row,
            row,
            row,
        ),
        (ANY,) * len(shapes) + (VMEM,) * 6,
        [
            pltpu.VMEM((ff, dim), bf16),
            pltpu.VMEM((dim, ff), bf16),
            pltpu.VMEM((dim, dim), bf16),
            pltpu.VMEM((dim, length), bf16),
            pltpu.VMEM((dim, length), bf16),
            pltpu.VMEM((length, ff), bf16),
            pltpu.VMEM((length, dim), f32),
            pltpu.VMEM((2, dim, 512), bf16),
            pltpu.VMEM((length, dim), bf16),
            pltpu.SemaphoreType.DMA((3,)),
            pltpu.SemaphoreType.DMA((2,)),
        ],
        (me, grad, low, slope, mid, normed, att, gain, *up_parts, *down_parts, *old),
        {8 + len(up_parts) + len(down_parts): 0} if old else None,
    )


def attn_back(me, d_att, qkv, lse, flag, normed, x, d_mid, gain, weight, others, at, last, outs, shapes, old):
    length, dim = x.shape
    colors, parts = weight
    extra = () if others is None else tuple(at)
    counts = (len(parts), len(old), len(shapes))
    before = 10 if extra else 9
    row = shaped((1, dim))
    scratch = [
        pltpu.VMEM((dim, 3 * dim), bf16),
        pltpu.VMEM((length, 3 * dim), bf16),
        pltpu.VMEM((dim, length), bf16),
        pltpu.VMEM((2, dim, 512), bf16),
        pltpu.SemaphoreType.DMA,
        pltpu.SemaphoreType.DMA((2,)),
    ]
    if extra:
        scratch += [pltpu.VMEM((dim, SIDE), bf16), pltpu.VMEM((SIDE, dim), f32)]
    return call(
        functools.partial(attn_back_body, colors, outs, counts, extra),
        "attn_back",
        [SMEM] + [VMEM] * (before - 1) + [ANY] * (len(parts) + len(old)),
        (*shapes, shaped((length, dim), bf16 if last else f32), row, row, row, row),
        (ANY,) * len(shapes) + (VMEM,) * 5,
        scratch,
        (me, d_att, qkv, lse, flag, normed, x, d_mid, gain)
        + ((others,) if extra else ())
        + tuple(parts)
        + tuple(old),
        {before + len(parts): 0} if old else None,
    )


def pack_body(a_ref, b_ref, out_ref):
    half = a_ref.shape[0]

    def step(i, carry):
        out_ref[i] = a_ref[i]
        out_ref[half + i] = b_ref[i]
        return carry

    lax.fori_loop(0, half, step, 0)


def pack(a, b):
    shape = (a.shape[0] * 2, *a.shape[1:])
    return call(pack_body, "pack", [VMEM] * 2, shaped(shape, bf16), VMEM, [], (a, b))


def merge_body(keep_ref, got_ref, low_ref, high_ref):
    half = low_ref.shape[0]

    def step(i, carry):
        low_ref[i] = keep_ref[i] + got_ref[i]
        high_ref[i] = keep_ref[half + i] + got_ref[half + i]
        return carry

    lax.fori_loop(0, half, step, 0)


def merge(keep, got):
    half = shaped((keep.shape[0] // 2, *keep.shape[1:]), bf16)
    return call(
        merge_body, "merge", [VMEM] * 2, (half, half), (VMEM, VMEM), [], (keep, got)
    )


def exchange(value, mask, n):
    return lax.ppermute(value, AXES, [(i, i ^ mask) for i in range(n)])


PARTNER = 2
NAMED = dict(x=1, y=4, b=8, a=24)


def other_masks(n):
    bits = n.bit_length() - 1
    return [1 << k for k in range(bits - 1, 1, -1)] + [1]


def span_table(masks):
    table = [0]
    for m in masks:
        table = table + [t ^ m for t in table]
    return tuple(table)


def owners_of(masks, me):
    return me ^ jnp.asarray(span_table(masks), jnp.int32)


def positions_of(masks, me):
    table = span_table(masks)
    inverse = [0] * len(table)
    for p, t in enumerate(table):
        inverse[t] = p
    return jnp.asarray(inverse, jnp.int32)[me ^ jnp.arange(len(table), dtype=jnp.int32)]


class Plan:
    def __init__(self, tied):
        self.actions = {}
        self.tied = tied
        self.last = None

    def ended(self, holder, key):
        self.last = (holder, key)

    def tie(self, value):
        if not self.tied or self.last is None:
            return value
        holder, key = self.last
        value, holder[key] = lax.optimization_barrier((value, holder[key]))
        return value

    def add(self, name, action):
        self.actions[name] = action

    def run(self, order):
        left = dict(self.actions)
        for name in order:
            weight_now[0] = PLACES.get(name, PLACE)
            left.pop(name)()
        assert not left, sorted(left)


def plan_gather(plan, name, own, masks, me, n, ready):
    state = dict(held=own[None])
    last = len(masks) - 1

    def start(k):
        state["got"] = exchange(plan.tie(state["held"]), masks[k], n)

    def finish(k):
        got = plan.tie(state["got"])
        if k < last:
            state["held"] = pack(state["held"], got)
            plan.ended(state, "held")
        else:
            state["end"] = got
            plan.ended(state, "end")

    def cross(k):
        state[k] = exchange(plan.tie(state["held" if k == 1 else "end"]), PARTNER, n)

    def crossed(k):
        state[k] = plan.tie(state[k])
        plan.ended(state, k)
        if k == 2:
            whole = masks + [PARTNER]
            parts = [state["held"], state["end"], state[1], state[2]]
            if n == BLOCKS:
                ready(span_table(whole), parts)
                plan.ended(parts, 3)
            else:
                joined = jnp.concatenate(parts, axis=0)[positions_of(whole, me)]
                joined = joined.reshape(4, BLOCKS // 4, -1, own.shape[1])
                ready(tuple(range(BLOCKS)), list(joined))

    for k in range(len(masks)):
        plan.add(name + k, functools.partial(start, k))
        plan.add(name + k + ENDS, functools.partial(finish, k))
    for k in (1, 2):
        plan.add(name + 19 + k, functools.partial(cross, k))
        plan.add(name + 19 + k + ENDS, functools.partial(crossed, k))


def plan_scatter(plan, name, given, masks, me, n, ready):
    state = {}

    def start(k):
        if k < 0:
            keep, send = given()
            if n != BLOCKS:
                whole = jnp.concatenate([keep, send], axis=0).reshape(n, -1, keep.shape[2])
                whole = whole[owners_of(masks[::-1] + [PARTNER], me)]
                keep, send = whole[: n // 2], whole[n // 2 :]
            state["keep"], state["send"] = keep, send
        mask = PARTNER if k < 0 else masks[k]
        state["got"] = exchange(plan.tie(state["send"]), mask, n)

    def finish(k):
        keep, got = state["keep"], plan.tie(state["got"])
        if k == len(masks) - 1:
            ready((keep.astype(f32) + got.astype(f32))[0])
            return
        state["keep"], state["send"] = merge(keep, got)
        plan.ended(state, "keep")

    for k in range(-1, len(masks)):
        plan.add(name + k + 1, functools.partial(start, k))
        plan.add(name + k + 1 + ENDS, functools.partial(finish, k))


WEIGHTS = ("qkv", "up", "down")
ENDS = 50
OUTWARD = 1000
TOKENS, COTANGENT, OUTPUT, INPUT_GRAD = 2000, 2001, 2002, 2003
GATHERED, SCATTERED = 2010, 2020
KERNELS = 3000


def number(w, l):
    return 100 * (2 * WEIGHTS.index(w) + l)


def plain_order(plan):
    def stage(a):
        if a >= KERNELS:
            return (1, LAYERS * (a - KERNELS >= 30), -(a % 10) if a >= KERNELS + 30 else a % 10, a)
        late = OUTWARD <= a < TOKENS or a % ENDS >= 2 and a >= TOKENS
        return (2 if late else 0, 0, 0, 0)

    return sorted(plan.actions, key=stage)


def per_device(
    n_devices,
    tokens,
    keep,
    norm_gain,
    norm_bias,
    qkv_weight,
    qv_bias,
    out_weight,
    out_bias,
    up_weight,
    up_bias,
    down_weight,
    down_bias,
    cotangent,
):
    n = n_devices
    seq_at = lax.axis_index("seq")
    me = lax.axis_index("dp") * 2 + seq_at
    n_images, local_len, model_dim = tokens.shape
    half_images = n_images // 2
    width = norm_gain.shape[2]
    ratio = up_bias.shape[1] // width
    hidden_dim = up_bias.shape[1] * n
    exact = n == BLOCKS
    who = (me if exact else jnp.zeros_like(me)).reshape(1)
    images = range(half_images)
    plan = Plan(exact and half_images == 1)

    positions = seq_at * local_len + lax.iota(jnp.int32, local_len)
    key_keep = ((keep == 1) | (positions < BUFFER)[None, :]).astype(bf16)

    def halves(value):
        low, high = value[:half_images], value[half_images:]
        mine = jnp.where(seq_at == 0, low, high)
        other = jnp.where(seq_at == 0, high, low)
        return mine, other

    def joined(mine, other):
        return jnp.where(
            seq_at == 0,
            jnp.concatenate([mine, other], axis=0),
            jnp.concatenate([other, mine], axis=0),
        )

    tok_mine, tok_other = halves(tokens)
    cot_mine, cot_other = halves(cotangent)
    keep_mine, keep_other = halves(key_keep)
    box = {}

    def start_tokens():
        below = ((0, 0), (0, 7), (0, model_dim - local_len))
        flags = jnp.pad(keep_other[:, None, :], below)
        sent = jnp.concatenate([tok_other, flags], axis=1)
        box["sent"] = exchange(plan.tie(sent), 1, n)

    def finish_tokens():
        got = plan.tie(box["sent"])
        box["tok"] = jnp.concatenate([tok_mine, got[:, :local_len]], axis=1)
        flags = jnp.concatenate([keep_mine, got[:, local_len, :local_len]], axis=1)
        box["keep"] = flags.astype(f32)[:, :, None]
        plan.ended(box, "tok")

    def start_cotangent():
        box["cot"] = exchange(plan.tie(cot_other), 1, n)

    def finish_cotangent():
        box["cot"] = jnp.concatenate([cot_mine, plan.tie(box["cot"])], axis=1)
        plan.ended(box, "cot")

    plan.add(TOKENS, start_tokens)
    plan.add(TOKENS + ENDS, finish_tokens)
    plan.add(COTANGENT, start_cotangent)
    plan.add(COTANGENT + ENDS, finish_cotangent)

    def columns(l):
        return [norm_gain[l, 0], norm_gain[l, 1], norm_bias[l, 0], norm_bias[l, 1]] + [
            qv_bias[l, 0],
            qv_bias[l, 1],
            out_bias[l],
            down_bias[l],
        ] + [up_bias[l, q * width : (q + 1) * width] for q in range(ratio)]

    stacked = jnp.stack(sum([columns(l) for l in range(LAYERS)], []))
    per_layer = stacked.shape[0] // LAYERS
    stacked = jnp.pad(stacked, ((0, SIDE - stacked.shape[0]), (0, 0))).T

    def ways(table, key):
        return [[NAMED[c] for c in way] for way in table[key]] if exact else [other_masks(n)]

    weights = {}
    packed = [exact and l == LAYERS - 1 for l in range(LAYERS)]
    chunks = dict(qkv=(0, 3), out=(3, 1), up=(4, ratio))
    tall = width * (4 + ratio)

    def receive(key, size, table, parts):
        weights[key] = (((0, size, table, 0, parts[0].shape[0], 0, not exact),), parts)

    def packed_colors(name, start=0):
        at, count = chunks[name]
        same = tuple(range(BLOCKS))
        return tuple(
            (start + c * model_dim, model_dim, same, 0, BLOCKS, width * (at + c), True)
            for c in range(count)
        )

    packed_kinds = dict(
        qkv=packed_colors("qkv"),
        up=packed_colors("up") + packed_colors("out", hidden_dim),
        down=((0, model_dim, tuple(range(BLOCKS)), 0, BLOCKS, tall, True),),
    )

    def start_packed(l):
        def rows(value):
            return value.reshape(width, -1, model_dim).swapaxes(0, 1).reshape(-1, model_dim)

        own = [rows(qkv_weight[l]), out_weight[l], rows(up_weight[l]), down_weight[l]]
        own = plan.tie(jnp.concatenate(own, axis=0))
        whole = lax.all_gather(own, AXES, axis=0, tiled=False)
        for w in WEIGHTS:
            weights[w + str(l)] = (packed_kinds[w], [whole])

    for l in range(LAYERS):
        if packed[l]:
            plan.add(GATHERED + l, functools.partial(start_packed, l))
            continue
        for w in WEIGHTS:
            key = w + str(l)
            if w == "qkv":
                own = qkv_weight[l]
                if l == 0:
                    own = jnp.concatenate([own, stacked], axis=1)
            elif w == "up":
                own = jnp.concatenate([up_weight[l], out_weight[l]], axis=1)
            else:
                own = down_weight[l]
            masks = ways(GATHER, key)[0]
            got = functools.partial(receive, key, own.shape[1])
            plan_gather(plan, number(w, l), own, masks, me, n, got)

    vectors = []

    def read_vectors():
        parts = weights["qkv0"][1]
        side = jnp.concatenate([part[:, :, 3 * model_dim :] for part in parts], axis=0)
        if exact:
            side = side[positions_of(ways(GATHER, "qkv0")[0] + [PARTNER], me)]
        side = side.reshape(model_dim, SIDE).T.astype(f32)
        for l in range(LAYERS):
            rows = side[l * per_layer : (l + 1) * per_layer]
            up_shift = rows[8:].reshape(ratio, n, width).transpose(1, 0, 2).reshape(1, -1)
            no_bias = jnp.zeros((1, model_dim), f32)
            vectors.append(
                dict(
                    gain=(rows[0:1], rows[1:2]),
                    shift=(rows[2:3], rows[3:4]),
                    qkv=jnp.concatenate([rows[4:5], no_bias, rows[5:6]], axis=1),
                    out=rows[6:7],
                    down=rows[7:8],
                    up=up_shift,
                )
            )

    saved = [[None] * LAYERS for _ in images]
    grads = {}
    vector_rows = [[None] * LAYERS for _ in images]
    outs, shapes = {}, {}
    for l in range(LAYERS):
        for w in WEIGHTS:
            key = w + str(l)
            if packed[l] and w != "down":
                outs[key] = packed_kinds[w]
                shapes[key] = [shaped((BLOCKS, tall + width, model_dim), bf16)]
                continue
            total = {"qkv": 3 * model_dim, "up": hidden_dim + model_dim, "down": model_dim}[w]
            total += SIDE if (w, l) == ("qkv", 0) else 0
            masks = ways(SCATTER, key)[0]
            table = span_table(masks[::-1] + [PARTNER]) if exact else tuple(range(BLOCKS))
            rows = (hidden_dim if w == "down" else model_dim) // BLOCKS
            outs[key] = ((0, total, table, 0, BLOCKS // 2, 0, not exact),)
            shapes[key] = [shaped((BLOCKS // 2, rows, total), bf16)] * 2

    def old_of(l, i):
        return [saved[i][l]["packed"]] if packed[l] and "packed" in saved[i][l] else []

    def gave(key, values, l, i):
        if packed[l] and len(values) == 1:
            saved[i][l]["packed"] = values[0]
            return
        grads[key] = values if key not in grads else [a + b for a, b in zip(grads[key], values)]

    def forward_one(l):
        if not vectors:
            read_vectors()
        v = vectors[l]
        for i in images:
            s = saved[i][l] = {}
            s["x"] = box["tok"][i] if l == 0 else saved[i][l - 1]["next"]
            s["normed"], s["qkv"], s["att"], s["lse"] = attn_fwd(
                plan.tie(who),
                s["x"],
                box["keep"][i],
                v["gain"][0],
                v["shift"][0],
                v["qkv"],
                weights["qkv" + str(l)],
            )
            plan.ended(s, "lse")

    def forward_two(l):
        v = vectors[l]
        for i in images:
            s = saved[i][l]
            s["mid"], s["normed_two"], s["hidden"], s["slope"] = mlp_up(
                plan.tie(who),
                s["x"],
                s["att"],
                v["out"],
                v["gain"][1],
                v["shift"][1],
                v["up"],
                weights["up" + str(l)],
            )
            plan.ended(s, "normed_two")

    def forward_three(l):
        for i in images:
            s = saved[i][l]
            s["next"] = mlp_down(
                plan.tie(who),
                s["mid"],
                s["hidden"],
                vectors[l]["down"],
                box["keep"][i],
                weights["down" + str(l)],
                l == LAYERS - 1,
            )
            plan.ended(s, "next")

    def back_one(l):
        for i in images:
            s = saved[i][l]
            if l == LAYERS - 1:
                s["grad"] = box["cot"][i].astype(f32) * box["keep"][i]
            else:
                s["grad"] = saved[i][l + 1]["d_x"]
            key = "down" + str(l)
            *values, s["low"], s["g_down"] = down_grad(
                plan.tie(who), s["grad"], s["hidden"], outs[key], shapes[key]
            )
            plan.ended(s, "low")
            gave(key, values, l, i)

    def back_two(l):
        for i in images:
            s = saved[i][l]
            key = "up" + str(l)
            *values, s["d_mid"], s["d_att"], g_up, g_gain, g_shift, g_out = mlp_back(
                plan.tie(who),
                s["grad"],
                s["low"],
                s["slope"],
                s["mid"],
                s["normed_two"],
                s["att"],
                vectors[l]["gain"][1],
                weights[key],
                weights["down" + str(l)],
                outs[key],
                shapes[key],
                old_of(l, i),
            )
            plan.ended(s, "d_mid")
            gave(key, values, l, i)
            up_rows = g_up.reshape(n, ratio, width).transpose(1, 0, 2).reshape(ratio, -1)
            blank = jnp.zeros_like(g_gain)
            vector_rows[i][l] = [blank, g_gain, blank, g_shift, blank, blank, g_out, s["g_down"]]
            vector_rows[i][l].append(up_rows)

    def back_three(l):
        for i in images:
            s = saved[i][l]
            others = None
            if l == 0:
                others = jnp.concatenate(sum(vector_rows[i], []), axis=0)
                others = jnp.pad(others, ((0, SIDE - others.shape[0]), (0, 0)))
            key = "qkv" + str(l)
            *values, s["d_x"], g_gain, g_shift, g_q, g_v = attn_back(
                plan.tie(who),
                s["d_att"],
                s["qkv"],
                s["lse"],
                box["keep"][i],
                s["normed"],
                s["x"],
                s["d_mid"],
                vectors[l]["gain"][0],
                weights[key],
                others,
                (0, 2, 4, 5),
                l == 0,
                outs[key],
                shapes[key],
                old_of(l, i),
            )
            plan.ended(s, "d_x")
            gave(key, values, l, i)
            rows = vector_rows[i][l]
            rows[0], rows[2], rows[4], rows[5] = g_gain, g_shift, g_q, g_v

    for l in range(LAYERS):
        steps = (forward_one, forward_two, forward_three, back_one, back_two, back_three)
        for at, step in enumerate(steps):
            plan.add(KERNELS + 10 * at + l, functools.partial(step, l))

    def start_back(name, key, l):
        whole = jnp.stack([saved[i][l][key] for i in images])
        box["mine" + name] = whole[:, :local_len]
        box[name] = exchange(plan.tie(whole[:, local_len:]), 1, n)

    def finish_back(name):
        box[name] = joined(box["mine" + name], plan.tie(box[name]))
        plan.ended(box, name)

    plan.add(OUTPUT, functools.partial(start_back, "out", "next", LAYERS - 1))
    plan.add(OUTPUT + ENDS, functools.partial(finish_back, "out"))
    plan.add(INPUT_GRAD, functools.partial(start_back, "dx", "d_x", 0))
    plan.add(INPUT_GRAD + ENDS, functools.partial(finish_back, "dx"))

    results = {}

    def take(key):
        return grads[key]

    def final(key, value):
        results[key] = value
        plan.ended(results, key)

    def start_scatter(l):
        whole = sum(saved[i][l]["packed"] for i in images[1:]) if len(images) > 1 else None
        whole = saved[0][l]["packed"] if whole is None else whole + saved[0][l]["packed"]
        whole = whole.reshape(-1, model_dim)
        got = lax.psum_scatter(whole, AXES, scatter_dimension=0, tiled=True).astype(f32)

        def wide(name):
            at, count = chunks[name]
            part = got[width * at : width * (at + count)]
            return part.reshape(count, width, model_dim).swapaxes(0, 1).reshape(width, -1)

        results["qkv" + str(l)] = wide("qkv")
        results["up" + str(l)] = jnp.concatenate([wide("up"), wide("out")], axis=1)

    for l in reversed(range(LAYERS)):
        if packed[l]:
            plan.add(SCATTERED + l, functools.partial(start_scatter, l))
        for w in ("down",) if packed[l] else ("down", "up", "qkv"):
            key = w + str(l)
            given = functools.partial(take, key)
            name = OUTWARD + number(w, l)
            masks = ways(SCATTER, key)[0]
            plan_scatter(plan, name, given, masks, me, n, functools.partial(final, key))

    plan.run(ORDER if plan.tied else plain_order(plan))

    g_qkv, g_up, g_down = ([results[w + str(l)] for l in range(LAYERS)] for w in WEIGHTS)
    vector_out = g_qkv[0][:, 3 * model_dim :].T

    def pick(at):
        return jnp.stack([vector_out[l * per_layer + at] for l in range(LAYERS)])

    return (
        box["out"],
        box["dx"].astype(f32),
        jnp.stack([pick(0), pick(1)], axis=1),
        jnp.stack([pick(2), pick(3)], axis=1),
        jnp.stack([g[:, : 3 * model_dim] for g in g_qkv]),
        jnp.stack([pick(4), pick(5)], axis=1),
        jnp.stack([g[:, hidden_dim:] for g in g_up]),
        pick(6),
        jnp.stack([g[:, :hidden_dim] for g in g_up]),
        jnp.concatenate([pick(8 + q) for q in range(ratio)], axis=1),
        jnp.stack(g_down),
        pick(7),
    )


GATHER = dict(
    up0=("abyx",),
    down0=("xaby",),
    qkv0=("byxa",),
)
SCATTER = dict(
    up0=("bxya",),
    down0=("yxba",),
    qkv0=("yxba",),
    down1=("xyab",),
)
PLACE = 10
PLACES = {3030: 9, 3040: 9, 3050: 9, 1550: 9, 1551: 9, 1552: 9, 1553: 9, 1554: 9, 1250: 9, 1251: 9, 1252: 9, 1253: 9, 1254: 9}
ORDER = (
    2011, 0, 200, 400, 2000, 2001, 50, 1, 250, 201, 450, 401, 2050, 2051, 51, 2, 251, 202, 451,
    402, 52, 3, 252, 203, 452, 403, 53, 21, 20, 220, 253, 221, 453, 421, 71, 420, 70, 3000, 270,
    271, 3010, 471, 470, 3020, 3001, 3011, 3031, 1500, 3041, 3051, 2021, 3030, 1400, 3040, 1200,
    1550, 1501, 1450, 1401, 1250, 1201, 3050, 2003, 1000, 3021, 1551, 1502, 1451, 1402, 1251,
    1202, 2053, 1050, 1001, 1552, 1503, 2002, 1452, 1403, 1252, 1203, 1051, 1002, 1553, 1504,
    2052, 1453, 1404, 1253, 1204, 1052, 1003, 1554, 1454, 1254, 1053, 1004, 1054,
)


def solution(mesh):
    n_devices = mesh.shape["dp"] * mesh.shape["seq"]
    rows = P(None, AXES, None)
    last = P(None, None, AXES)
    flat = P(None, AXES)
    batch = P("dp", "seq", None)

    def body(*args):
        return per_device(n_devices, *args)

    return jax.shard_map(
        body,
        mesh=mesh,
        in_specs=(
            batch,
            P("dp", "seq"),
            last,
            last,
            rows,
            last,
            rows,
            flat,
            rows,
            flat,
            rows,
            flat,
            batch,
        ),
        out_specs=(batch, batch, last, last, rows, last, rows, flat, rows, flat, rows, flat),
        check_vma=False,
    )
```

```python
import functools

import jax
import jax.numpy as jnp
from jax import lax
from jax.experimental import pallas as pl
from jax.experimental.pallas import tpu as pltpu
from jax.sharding import PartitionSpec as P

HEAD = 64
BUFFER = 64
LAYERS = 2
AXES = ("dp", "seq")
BLOCKS = 32
SIDE = 128

masked_score = -1e30
f32 = jnp.float32
bf16 = jnp.bfloat16
INV_SQRT2 = 0.7071067811865476
INV_SQRT2PI = 0.3989422804014327

VMEM = pl.BlockSpec(memory_space=pltpu.VMEM)
SMEM = pl.BlockSpec(memory_space=pltpu.SMEM)
ANY = pl.BlockSpec(memory_space=pl.ANY)
weight_now = [10]
VMEM_LIMIT = 58 * 1024 * 1024


def mm(a, b):
    return lax.dot_general(a, b, (((1,), (0,)), ((), ())), preferred_element_type=f32)


def mm_nt(a, b):
    return lax.dot_general(a, b, (((1,), (1,)), ((), ())), preferred_element_type=f32)


def mm_tn(a, b):
    return lax.dot_general(a, b, (((0,), (0,)), ((), ())), preferred_element_type=f32)


def centred(x):
    mean = jnp.mean(x, axis=-1, keepdims=True)
    c = x - mean
    r = lax.rsqrt(jnp.mean(c * c, axis=-1, keepdims=True) + 1e-06)
    return c * r, r


def norm_back(d, n, r, gain):
    e = d * gain
    mean_e = jnp.mean(e, axis=-1, keepdims=True)
    mean_en = jnp.mean(e * n, axis=-1, keepdims=True)
    return r * (e - mean_e - n * mean_en)


def columns_sum(v):
    return jnp.sum(v, axis=0, keepdims=True)


def fetch(colors, parts, me, dst, sem, start=0):
    stop = start + dst.shape[1]
    for first, width, table, at, per, base, fixed in colors:
        low, high = max(start, first), min(stop, first + width)
        if low >= high:
            continue
        rows = dst.shape[0] // len(table)
        for p, offset in enumerate(table):
            owner = p if fixed else me ^ offset
            to_rows = pl.ds(pl.multiple_of(owner * rows, rows), rows)
            cols = pl.ds(low - first, high - low)
            src = parts[at + p // per].at[p % per, pl.ds(base, rows), cols]
            to = dst.at[to_rows, pl.ds(low - start, high - low)]
            pltpu.make_async_copy(src, to, sem).start()


def arrived(dst, sem):
    pltpu.make_async_copy(dst, dst, sem).wait()


def spread(src, out, me, arrays, sem, start):
    first, _, table, at, per, base, fixed = out
    width = src.shape[1]
    rows = src.shape[0] // len(table)
    for p, offset in enumerate(table):
        owner = p if fixed else me ^ offset
        from_rows = pl.ds(pl.multiple_of(owner * rows, rows), rows)
        to = arrays[at + p // per].at[p % per, pl.ds(base, rows), pl.ds(start, width)]
        pltpu.make_async_copy(src.at[from_rows, :], to, sem).start()


def holds(outs, column):
    return [o for o in outs if o[0] <= column < o[0] + o[1]][0]


def attn_fwd_body(colors, many, me_ref, x_ref, flag_ref, gain_ref, shift_ref, bias_ref, *refs):
    parts, refs = refs[:many], refs[many:]
    normed_ref, qkv_ref, att_ref, lse_ref, w, sem = refs
    dim = x_ref.shape[1]
    fetch(colors, parts, me_ref[0], w, sem)
    n, _ = centred(x_ref[...].astype(f32))
    normed_ref[...] = (n * gain_ref[...] + shift_ref[...]).astype(bf16)
    arrived(w, sem)

    def project(c, carry):
        cols = pl.ds(pl.multiple_of(c * 512, 512), 512)
        qkv_ref[:, cols] = (mm(normed_ref[...], w[:, cols]) + bias_ref[:, cols]).astype(bf16)
        return carry

    lax.fori_loop(0, 3 * dim // 512, project, 0)
    allowed = flag_ref[...] > 0
    scale = HEAD ** (-0.5)

    def two_heads(hp, carry):
        base = pl.multiple_of(hp * 128, 128)
        q2 = qkv_ref[:, pl.ds(base, 128)]
        k2 = qkv_ref[:, pl.ds(pl.multiple_of(dim + hp * 128, 128), 128)]
        v2 = qkv_ref[:, pl.ds(pl.multiple_of(2 * dim + hp * 128, 128), 128)]
        outs = []
        for s in range(2):
            cut = slice(s * HEAD, (s + 1) * HEAD)
            score = jnp.where(allowed, mm_nt(k2[:, cut], q2[:, cut]) * scale, masked_score)
            top = jnp.max(score, axis=0, keepdims=True)
            e = jnp.exp(score - top)
            total = jnp.sum(e, axis=0, keepdims=True)
            probs = (e * (1.0 / total)).astype(bf16)
            lse_ref[pl.ds(2 * hp + s, 1), :] = top + jnp.log(total)
            outs.append(mm_tn(probs, v2[:, cut]))
        att_ref[:, pl.ds(base, 128)] = jnp.concatenate(outs, axis=1).astype(bf16)
        return carry

    lax.fori_loop(0, dim // 128, two_heads, 0)


def mlp_up_body(colors, many, me_ref, x_ref, att_ref, ob_ref, gain_ref, shift_ref, ub_ref, *refs):
    parts, refs = refs[:many], refs[many:]
    mid_ref, normed_ref, hidden_ref, slope_ref, w_out, w_up, sem = refs
    ff = ub_ref.shape[1]
    fetch(colors, parts, me_ref[0], w_out, sem.at[0], ff)
    fetch(colors, parts, me_ref[0], w_up, sem.at[1])
    arrived(w_out, sem.at[0])
    mid = x_ref[...].astype(f32) + mm(att_ref[...], w_out[...]) + ob_ref[...]
    mid_ref[...] = mid
    n, _ = centred(mid)
    normed_ref[...] = (n * gain_ref[...] + shift_ref[...]).astype(bf16)
    arrived(w_up, sem.at[1])

    def step(c, carry):
        cols = pl.ds(pl.multiple_of(c * 512, 512), 512)
        u = mm(normed_ref[...], w_up[:, cols]) + ub_ref[:, cols]
        phi = 0.5 + 0.5 * lax.erf(u * INV_SQRT2)
        hidden_ref[:, cols] = (u * phi).astype(bf16)
        slope_ref[:, cols] = phi + u * (INV_SQRT2PI * jnp.exp(-0.5 * u * u))
        return carry

    lax.fori_loop(0, ff // 512, step, 0)


def mlp_down_body(colors, many, last, me_ref, mid_ref, hidden_ref, db_ref, flag_ref, *refs):
    parts, refs = refs[:many], refs[many:]
    out_ref, w, sem = refs
    fetch(colors, parts, me_ref[0], w, sem)
    arrived(w, sem)
    for c in range(0, w.shape[1], 512):
        cols = slice(c, c + 512)
        y = mid_ref[:, cols] + mm(hidden_ref[...], w[:, cols]) + db_ref[:, cols]
        if last:
            y = (y * flag_ref[...]).astype(bf16)
        out_ref[:, cols] = y


def down_grad_body(outs, many, me_ref, grad_ref, hidden_ref, *refs):
    arrays, refs = refs[:many], refs[many:]
    low_ref, sum_ref, perm, tile, sem = refs
    me = me_ref[0]
    grad = grad_ref[...]
    low_ref[...] = grad.astype(bf16)
    sum_ref[...] = columns_sum(grad)
    group = 4
    ((first, width, table, at, per, base, fixed),) = outs
    rows = hidden_ref.shape[1] // len(table)
    for p, offset in enumerate(table):
        owner = pl.ds(pl.multiple_of((p if fixed else me ^ offset) * rows, rows), rows)
        perm[:, p * rows : (p + 1) * rows] = hidden_ref[:, owner]
    pending = [None, None]
    for g in reversed(range(len(table) // group)):
        slot = g % 2
        if pending[slot] is not None:
            pending[slot].wait()
        cut = slice(g * group * rows, (g + 1) * group * rows)
        block = mm_tn(perm[:, cut], low_ref[...])
        tile[slot] = block.astype(bf16).reshape(tile.shape[1:])
        b0 = g * group
        to = arrays[at + b0 // per].at[pl.ds(b0 % per, group), pl.ds(base, rows)]
        pending[slot] = pltpu.make_async_copy(tile.at[slot], to, sem.at[slot])
        pending[slot].start()
    for copy in pending:
        copy.wait()


def mlp_back_body(ups, downs, outs, many, me_ref, grad_ref, low_ref, slope_ref, mid_ref, *refs):
    normed_ref, att_ref, gain_ref, refs = refs[0], refs[1], refs[2], refs[3:]
    many_up, many_down, many_in, many_out = many
    up_parts, refs = refs[:many_up], refs[many_up:]
    down_parts, refs = refs[:many_down], refs[many_down:]
    refs = refs[many_in:]
    halves, refs = refs[:many_out], refs[many_out:]
    d_mid_ref, d_att_ref, g_up_ref, g_gain, g_shift, g_out, refs = (*refs[:6], refs[6:])
    w_down, w_up, w_out, turned, turned_att, d_low_ref, acc, tile, low_mid, sem, out_sem = refs
    me = me_ref[0]
    ff, dim = w_down.shape
    fetch(downs, down_parts, me, w_down, sem.at[0])
    fetch(ups, up_parts, me, w_up, sem.at[1])
    fetch(ups, up_parts, me, w_out, sem.at[2], ff)
    turned[...] = normed_ref[...].T
    turned_att[...] = att_ref[...].T
    acc[...] = jnp.zeros_like(acc)
    arrived(w_down, sem.at[0])

    def first_step(c, carry):
        cols = pl.ds(pl.multiple_of(c * 512, 512), 512)
        d_up = mm_nt(low_ref[...], w_down[cols, :]) * slope_ref[:, cols]
        g_up_ref[:, cols] = columns_sum(d_up)
        d_low_ref[:, cols] = d_up.astype(bf16)
        return carry

    lax.fori_loop(0, ff // 512, first_step, 0)
    arrived(w_up, sem.at[1])

    def flush(slot):
        pltpu.make_async_copy(tile.at[slot], tile.at[slot], out_sem.at[slot]).wait()

    for out in outs:
        first, width = out[:2]
        stop = min(first + width, ff)

        def step(c, carry, out=out, first=first):
            start = pl.multiple_of(c * 512, 512)
            cols = pl.ds(start, 512)
            slot = lax.rem(c, 2)

            @pl.when(c >= 2)
            def _():
                flush(slot)

            tile[slot] = mm(turned[...], d_low_ref[:, cols]).astype(bf16)
            local = pl.multiple_of(start - first, 512)
            spread(tile.at[slot], out, me, halves, out_sem.at[slot], local)
            acc[...] += mm_nt(d_low_ref[:, cols], w_up[:, cols])
            return carry

        lax.fori_loop(first // 512, stop // 512, step, 0)
    n, r = centred(mid_ref[...])
    d = acc[...]
    g_gain[...] = columns_sum(d * n)
    g_shift[...] = columns_sum(d)
    d_mid = grad_ref[...] + norm_back(d, n, r, gain_ref[...])
    d_mid_ref[...] = d_mid
    g_out[...] = columns_sum(d_mid)
    low_mid[...] = d_mid.astype(bf16)
    arrived(w_out, sem.at[2])
    for c in range(dim // 512):
        flush(c % 2)
        tile[c % 2] = mm(turned_att[...], low_mid[:, c * 512 : (c + 1) * 512]).astype(bf16)
        start = ff + c * 512
        out = holds(outs, start)
        spread(tile.at[c % 2], out, me, halves, out_sem.at[c % 2], start - out[0])
    d_att_ref[...] = mm_nt(low_mid[...], w_out[...]).astype(bf16)
    flush(0)
    flush(1)


def attn_back_body(colors, outs, counts, extra, me_ref, d_att_ref, qkv_ref, lse_ref, flag_ref, *refs):
    many, many_in, many_out = counts
    normed_ref, x_ref, d_mid_ref, gain_ref, refs = *refs[:4], refs[4:]
    if extra:
        others_ref, refs = refs[0], refs[1:]
    parts, refs = refs[:many], refs[many:]
    refs = refs[many_in:]
    halves, refs = refs[:many_out], refs[many_out:]
    d_x_ref, g_gain, g_shift, g_query, g_value, refs = (*refs[:5], refs[5:])
    if extra:
        w, d_qkv, turned, tile, sem, out_sem, column, wide = refs
    else:
        w, d_qkv, turned, tile, sem, out_sem = refs
    me = me_ref[0]
    dim = x_ref.shape[1]
    fetch(colors, parts, me, w, sem)
    turned[...] = normed_ref[...].T
    allowed = flag_ref[...] > 0
    scale = HEAD ** (-0.5)

    def two_heads(hp, carry):
        at_q = pl.ds(pl.multiple_of(hp * 128, 128), 128)
        at_k = pl.ds(pl.multiple_of(dim + hp * 128, 128), 128)
        at_v = pl.ds(pl.multiple_of(2 * dim + hp * 128, 128), 128)
        q2, k2, v2, d2 = qkv_ref[:, at_q], qkv_ref[:, at_k], qkv_ref[:, at_v], d_att_ref[:, at_q]
        dq, dk, dv = [], [], []
        for s in range(2):
            cut = slice(s * HEAD, (s + 1) * HEAD)
            q, k, v, d = q2[:, cut], k2[:, cut], v2[:, cut], d2[:, cut]
            score = jnp.where(allowed, mm_nt(k, q) * scale, masked_score)
            probs = jnp.exp(score - lse_ref[pl.ds(2 * hp + s, 1), :])
            dv.append(mm(probs.astype(bf16), d))
            d_probs = mm_nt(v, d)
            inner = jnp.sum(probs * d_probs, axis=0, keepdims=True)
            d_score = (probs * (d_probs - inner)).astype(bf16)
            dq.append(mm_tn(d_score, k) * scale)
            dk.append(mm(d_score, q) * scale)
        d_qkv[:, at_q] = jnp.concatenate(dq, axis=1).astype(bf16)
        d_qkv[:, at_k] = jnp.concatenate(dk, axis=1).astype(bf16)
        d_qkv[:, at_v] = jnp.concatenate(dv, axis=1).astype(bf16)
        return carry

    lax.fori_loop(0, dim // 128, two_heads, 0)

    def flush(slot):
        pltpu.make_async_copy(tile.at[slot], tile.at[slot], out_sem.at[slot]).wait()

    for c in range(3 * dim // 512):
        if c >= 2:
            flush(c % 2)
        tile[c % 2] = mm(turned[...], d_qkv[:, c * 512 : (c + 1) * 512]).astype(bf16)
        out = holds(outs, c * 512)
        spread(tile.at[c % 2], out, me, halves, out_sem.at[c % 2], c * 512 - out[0])
    g_query[...] = columns_sum(d_qkv[:, :dim].astype(f32))
    g_value[...] = columns_sum(d_qkv[:, 2 * dim :].astype(f32))
    arrived(w, sem)
    d = mm_nt(d_qkv[...], w[...])
    n, r = centred(x_ref[...].astype(f32))
    g_gain[...] = columns_sum(d * n)
    g_shift[...] = columns_sum(d)
    d_x_ref[...] = (d_mid_ref[...] + norm_back(d, n, r, gain_ref[...])).astype(d_x_ref.dtype)
    if extra:
        wide[...] = others_ref[...]
        for at, row in zip(extra, (g_gain, g_shift, g_query, g_value)):
            wide[at : at + 1, :] = row[...]
        column[...] = wide[...].T.astype(bf16)
        spread(column, outs[-1], me, halves, sem, 3 * dim - outs[-1][0])
        arrived(column, sem)
    flush(0)
    flush(1)


def shaped(shape, dtype=f32):
    return jax.ShapeDtypeStruct(shape, dtype)


def call(body, name, in_specs, out_shapes, out_specs, scratch, args, aliases=None):
    return pl.pallas_call(
        body,
        in_specs=in_specs,
        out_specs=out_specs,
        out_shape=out_shapes,
        scratch_shapes=scratch,
        input_output_aliases=aliases or {},
        compiler_params=pltpu.CompilerParams(vmem_limit_bytes=VMEM_LIMIT),
        cost_estimate=pl.CostEstimate(
            flops=10 ** weight_now[0], bytes_accessed=0, transcendentals=0
        ),
        name=name,
    )(*args)


def attn_fwd(me, x, flag, gain, shift, bias, weight):
    length, dim = x.shape
    colors, parts = weight
    return call(
        functools.partial(attn_fwd_body, colors, len(parts)),
        "attn_fwd",
        [SMEM] + [VMEM] * 5 + [ANY] * len(parts),
        (
            shaped((length, dim), bf16),
            shaped((length, 3 * dim), bf16),
            shaped((length, dim), bf16),
            shaped((dim // HEAD, length)),
        ),
        (VMEM,) * 4,
        [pltpu.VMEM((dim, 3 * dim), bf16), pltpu.SemaphoreType.DMA],
        (me, x, flag, gain, shift, bias, *parts),
    )


def mlp_up(me, x, att, out_bias, gain, shift, up_bias, weight):
    length, dim = x.shape
    ff = up_bias.shape[1]
    colors, parts = weight
    return call(
        functools.partial(mlp_up_body, colors, len(parts)),
        "mlp_up",
        [SMEM] + [VMEM] * 6 + [ANY] * len(parts),
        (
            shaped((length, dim)),
            shaped((length, dim), bf16),
            shaped((length, ff), bf16),
            shaped((length, ff)),
        ),
        (VMEM,) * 4,
        [
            pltpu.VMEM((dim, dim), bf16),
            pltpu.VMEM((dim, ff), bf16),
            pltpu.SemaphoreType.DMA((2,)),
        ],
        (me, x, att, out_bias, gain, shift, up_bias, *parts),
    )


def mlp_down(me, mid, hidden, down_bias, flag, weight, last):
    length, dim = mid.shape
    ff = hidden.shape[1]
    colors, parts = weight
    return call(
        functools.partial(mlp_down_body, colors, len(parts), last),
        "mlp_down",
        [SMEM] + [VMEM] * 4 + [ANY] * len(parts),
        shaped((length, dim), bf16 if last else f32),
        VMEM,
        [pltpu.VMEM((ff, dim), bf16), pltpu.SemaphoreType.DMA],
        (me, mid, hidden, down_bias, flag, *parts),
    )


def down_grad(me, grad, hidden, outs, shapes):
    length, dim = grad.shape
    ff = hidden.shape[1]
    return call(
        functools.partial(down_grad_body, outs, len(shapes)),
        "down_grad",
        [SMEM, VMEM, VMEM],
        (*shapes, shaped((length, dim), bf16), shaped((1, dim))),
        (ANY,) * len(shapes) + (VMEM, VMEM),
        [
            pltpu.VMEM((length, ff), bf16),
            pltpu.VMEM((2, 4, ff // BLOCKS, dim), bf16),
            pltpu.SemaphoreType.DMA((2,)),
        ],
        (me, grad, hidden),
    )


def mlp_back(me, grad, low, slope, mid, normed, att, gain, up_weight, down_weight, outs, shapes, old):
    length, dim = grad.shape
    ff = slope.shape[1]
    ups, up_parts = up_weight
    downs, down_parts = down_weight
    many = (len(up_parts), len(down_parts), len(old), len(shapes))
    row = shaped((1, dim))
    return call(
        functools.partial(mlp_back_body, ups, downs, outs, many),
        "mlp_back",
        [SMEM] + [VMEM] * 7 + [ANY] * (len(up_parts) + len(down_parts) + len(old)),
        (
            *shapes,
            shaped((length, dim)),
            shaped((length, dim), bf16),
            shaped((1, ff)),
            row,
            row,
            row,
        ),
        (ANY,) * len(shapes) + (VMEM,) * 6,
        [
            pltpu.VMEM((ff, dim), bf16),
            pltpu.VMEM((dim, ff), bf16),
            pltpu.VMEM((dim, dim), bf16),
            pltpu.VMEM((dim, length), bf16),
            pltpu.VMEM((dim, length), bf16),
            pltpu.VMEM((length, ff), bf16),
            pltpu.VMEM((length, dim), f32),
            pltpu.VMEM((2, dim, 512), bf16),
            pltpu.VMEM((length, dim), bf16),
            pltpu.SemaphoreType.DMA((3,)),
            pltpu.SemaphoreType.DMA((2,)),
        ],
        (me, grad, low, slope, mid, normed, att, gain, *up_parts, *down_parts, *old),
        {8 + len(up_parts) + len(down_parts): 0} if old else None,
    )


def attn_back(me, d_att, qkv, lse, flag, normed, x, d_mid, gain, weight, others, at, last, outs, shapes, old):
    length, dim = x.shape
    colors, parts = weight
    extra = () if others is None else tuple(at)
    counts = (len(parts), len(old), len(shapes))
    before = 10 if extra else 9
    row = shaped((1, dim))
    scratch = [
        pltpu.VMEM((dim, 3 * dim), bf16),
        pltpu.VMEM((length, 3 * dim), bf16),
        pltpu.VMEM((dim, length), bf16),
        pltpu.VMEM((2, dim, 512), bf16),
        pltpu.SemaphoreType.DMA,
        pltpu.SemaphoreType.DMA((2,)),
    ]
    if extra:
        scratch += [pltpu.VMEM((dim, SIDE), bf16), pltpu.VMEM((SIDE, dim), f32)]
    return call(
        functools.partial(attn_back_body, colors, outs, counts, extra),
        "attn_back",
        [SMEM] + [VMEM] * (before - 1) + [ANY] * (len(parts) + len(old)),
        (*shapes, shaped((length, dim), bf16 if last else f32), row, row, row, row),
        (ANY,) * len(shapes) + (VMEM,) * 5,
        scratch,
        (me, d_att, qkv, lse, flag, normed, x, d_mid, gain)
        + ((others,) if extra else ())
        + tuple(parts)
        + tuple(old),
        {before + len(parts): 0} if old else None,
    )


def pack_body(a_ref, b_ref, out_ref):
    half = a_ref.shape[0]

    def step(i, carry):
        out_ref[i] = a_ref[i]
        out_ref[half + i] = b_ref[i]
        return carry

    lax.fori_loop(0, half, step, 0)


def pack(a, b):
    shape = (a.shape[0] * 2, *a.shape[1:])
    return call(pack_body, "pack", [VMEM] * 2, shaped(shape, bf16), VMEM, [], (a, b))


def merge_body(keep_ref, got_ref, low_ref, high_ref):
    half = low_ref.shape[0]

    def step(i, carry):
        low_ref[i] = keep_ref[i] + got_ref[i]
        high_ref[i] = keep_ref[half + i] + got_ref[half + i]
        return carry

    lax.fori_loop(0, half, step, 0)


def merge(keep, got):
    half = shaped((keep.shape[0] // 2, *keep.shape[1:]), bf16)
    return call(
        merge_body, "merge", [VMEM] * 2, (half, half), (VMEM, VMEM), [], (keep, got)
    )


def exchange(value, mask, n):
    return lax.ppermute(value, AXES, [(i, i ^ mask) for i in range(n)])


PARTNER = 2
NAMED = dict(x=1, y=4, b=8, a=24)


def other_masks(n):
    bits = n.bit_length() - 1
    return [1 << k for k in range(bits - 1, 1, -1)] + [1]


def span_table(masks):
    table = [0]
    for m in masks:
        table = table + [t ^ m for t in table]
    return tuple(table)


def owners_of(masks, me):
    return me ^ jnp.asarray(span_table(masks), jnp.int32)


def positions_of(masks, me):
    table = span_table(masks)
    inverse = [0] * len(table)
    for p, t in enumerate(table):
        inverse[t] = p
    return jnp.asarray(inverse, jnp.int32)[me ^ jnp.arange(len(table), dtype=jnp.int32)]


class Plan:
    def __init__(self, tied):
        self.actions = {}
        self.tied = tied
        self.last = None

    def ended(self, holder, key):
        self.last = (holder, key)

    def tie(self, value):
        if not self.tied or self.last is None:
            return value
        holder, key = self.last
        value, holder[key] = lax.optimization_barrier((value, holder[key]))
        return value

    def add(self, name, action):
        self.actions[name] = action

    def run(self, order):
        left = dict(self.actions)
        for name in order:
            weight_now[0] = PLACES.get(name, PLACE)
            left.pop(name)()
        assert not left, sorted(left)


def plan_gather(plan, name, own, masks, me, n, ready):
    state = dict(held=own[None])
    last = len(masks) - 1

    def start(k):
        state["got"] = exchange(plan.tie(state["held"]), masks[k], n)

    def finish(k):
        got = plan.tie(state["got"])
        if k < last:
            state["held"] = pack(state["held"], got)
            plan.ended(state, "held")
        else:
            state["end"] = got
            plan.ended(state, "end")

    def cross(k):
        state[k] = exchange(plan.tie(state["held" if k == 1 else "end"]), PARTNER, n)

    def crossed(k):
        state[k] = plan.tie(state[k])
        plan.ended(state, k)
        if k == 2:
            whole = masks + [PARTNER]
            parts = [state["held"], state["end"], state[1], state[2]]
            if n == BLOCKS:
                ready(span_table(whole), parts)
                plan.ended(parts, 3)
            else:
                joined = jnp.concatenate(parts, axis=0)[positions_of(whole, me)]
                joined = joined.reshape(4, BLOCKS // 4, -1, own.shape[1])
                ready(tuple(range(BLOCKS)), list(joined))

    for k in range(len(masks)):
        plan.add(name + k, functools.partial(start, k))
        plan.add(name + k + ENDS, functools.partial(finish, k))
    for k in (1, 2):
        plan.add(name + 19 + k, functools.partial(cross, k))
        plan.add(name + 19 + k + ENDS, functools.partial(crossed, k))


def plan_scatter(plan, name, given, masks, me, n, ready):
    state = {}

    def start(k):
        if k < 0:
            keep, send = given()
            if n != BLOCKS:
                whole = jnp.concatenate([keep, send], axis=0).reshape(n, -1, keep.shape[2])
                whole = whole[owners_of(masks[::-1] + [PARTNER], me)]
                keep, send = whole[: n // 2], whole[n // 2 :]
            state["keep"], state["send"] = keep, send
        mask = PARTNER if k < 0 else masks[k]
        state["got"] = exchange(plan.tie(state["send"]), mask, n)

    def finish(k):
        keep, got = state["keep"], plan.tie(state["got"])
        if k == len(masks) - 1:
            ready((keep.astype(f32) + got.astype(f32))[0])
            return
        state["keep"], state["send"] = merge(keep, got)
        plan.ended(state, "keep")

    for k in range(-1, len(masks)):
        plan.add(name + k + 1, functools.partial(start, k))
        plan.add(name + k + 1 + ENDS, functools.partial(finish, k))


WEIGHTS = ("qkv", "up", "down")
ENDS = 50
OUTWARD = 1000
TOKENS, COTANGENT, OUTPUT, INPUT_GRAD = 2000, 2001, 2002, 2003
GATHERED, SCATTERED = 2010, 2020
KERNELS = 3000


def number(w, l):
    return 100 * (2 * WEIGHTS.index(w) + l)


def plain_order(plan):
    def stage(a):
        if a >= KERNELS:
            return (1, LAYERS * (a - KERNELS >= 30), -(a % 10) if a >= KERNELS + 30 else a % 10, a)
        late = OUTWARD <= a < TOKENS or a % ENDS >= 2 and a >= TOKENS
        return (2 if late else 0, 0, 0, 0)

    return sorted(plan.actions, key=stage)


def per_device(
    n_devices,
    tokens,
    keep,
    norm_gain,
    norm_bias,
    qkv_weight,
    qv_bias,
    out_weight,
    out_bias,
    up_weight,
    up_bias,
    down_weight,
    down_bias,
    cotangent,
):
    n = n_devices
    seq_at = lax.axis_index("seq")
    me = lax.axis_index("dp") * 2 + seq_at
    n_images, local_len, model_dim = tokens.shape
    half_images = n_images // 2
    width = norm_gain.shape[2]
    ratio = up_bias.shape[1] // width
    hidden_dim = up_bias.shape[1] * n
    exact = n == BLOCKS
    who = (me if exact else jnp.zeros_like(me)).reshape(1)
    images = range(half_images)
    plan = Plan(exact and half_images == 1)

    positions = seq_at * local_len + lax.iota(jnp.int32, local_len)
    key_keep = ((keep == 1) | (positions < BUFFER)[None, :]).astype(bf16)

    def halves(value):
        low, high = value[:half_images], value[half_images:]
        mine = jnp.where(seq_at == 0, low, high)
        other = jnp.where(seq_at == 0, high, low)
        return mine, other

    def joined(mine, other):
        return jnp.where(
            seq_at == 0,
            jnp.concatenate([mine, other], axis=0),
            jnp.concatenate([other, mine], axis=0),
        )

    tok_mine, tok_other = halves(tokens)
    cot_mine, cot_other = halves(cotangent)
    keep_mine, keep_other = halves(key_keep)
    box = {}

    def start_tokens():
        below = ((0, 0), (0, 7), (0, model_dim - local_len))
        flags = jnp.pad(keep_other[:, None, :], below)
        sent = jnp.concatenate([tok_other, flags], axis=1)
        box["sent"] = exchange(plan.tie(sent), 1, n)

    def finish_tokens():
        got = plan.tie(box["sent"])
        box["tok"] = jnp.concatenate([tok_mine, got[:, :local_len]], axis=1)
        flags = jnp.concatenate([keep_mine, got[:, local_len, :local_len]], axis=1)
        box["keep"] = flags.astype(f32)[:, :, None]
        plan.ended(box, "tok")

    def start_cotangent():
        box["cot"] = exchange(plan.tie(cot_other), 1, n)

    def finish_cotangent():
        box["cot"] = jnp.concatenate([cot_mine, plan.tie(box["cot"])], axis=1)
        plan.ended(box, "cot")

    plan.add(TOKENS, start_tokens)
    plan.add(TOKENS + ENDS, finish_tokens)
    plan.add(COTANGENT, start_cotangent)
    plan.add(COTANGENT + ENDS, finish_cotangent)

    def columns(l):
        return [norm_gain[l, 0], norm_gain[l, 1], norm_bias[l, 0], norm_bias[l, 1]] + [
            qv_bias[l, 0],
            qv_bias[l, 1],
            out_bias[l],
            down_bias[l],
        ] + [up_bias[l, q * width : (q + 1) * width] for q in range(ratio)]

    stacked = jnp.stack(sum([columns(l) for l in range(LAYERS)], []))
    per_layer = stacked.shape[0] // LAYERS
    stacked = jnp.pad(stacked, ((0, SIDE - stacked.shape[0]), (0, 0))).T

    def ways(table, key):
        return [[NAMED[c] for c in way] for way in table[key]] if exact else [other_masks(n)]

    weights = {}
    packed = [exact and l == LAYERS - 1 for l in range(LAYERS)]
    chunks = dict(qkv=(0, 3), out=(3, 1), up=(4, ratio))
    tall = width * (4 + ratio)

    def receive(key, size, table, parts):
        weights[key] = (((0, size, table, 0, parts[0].shape[0], 0, not exact),), parts)

    def packed_colors(name, start=0):
        at, count = chunks[name]
        same = tuple(range(BLOCKS))
        return tuple(
            (start + c * model_dim, model_dim, same, 0, BLOCKS, width * (at + c), True)
            for c in range(count)
        )

    packed_kinds = dict(
        qkv=packed_colors("qkv"),
        up=packed_colors("up") + packed_colors("out", hidden_dim),
        down=((0, model_dim, tuple(range(BLOCKS)), 0, BLOCKS, tall, True),),
    )

    def start_packed(l):
        def rows(value):
            return value.reshape(width, -1, model_dim).swapaxes(0, 1).reshape(-1, model_dim)

        own = [rows(qkv_weight[l]), out_weight[l], rows(up_weight[l]), down_weight[l]]
        own = plan.tie(jnp.concatenate(own, axis=0))
        whole = lax.all_gather(own, AXES, axis=0, tiled=False)
        for w in WEIGHTS:
            weights[w + str(l)] = (packed_kinds[w], [whole])

    for l in range(LAYERS):
        if packed[l]:
            plan.add(GATHERED + l, functools.partial(start_packed, l))
            continue
        for w in WEIGHTS:
            key = w + str(l)
            if w == "qkv":
                own = qkv_weight[l]
                if l == 0:
                    own = jnp.concatenate([own, stacked], axis=1)
            elif w == "up":
                own = jnp.concatenate([up_weight[l], out_weight[l]], axis=1)
            else:
                own = down_weight[l]
            masks = ways(GATHER, key)[0]
            got = functools.partial(receive, key, own.shape[1])
            plan_gather(plan, number(w, l), own, masks, me, n, got)

    vectors = []

    def read_vectors():
        parts = weights["qkv0"][1]
        side = jnp.concatenate([part[:, :, 3 * model_dim :] for part in parts], axis=0)
        if exact:
            side = side[positions_of(ways(GATHER, "qkv0")[0] + [PARTNER], me)]
        side = side.reshape(model_dim, SIDE).T.astype(f32)
        for l in range(LAYERS):
            rows = side[l * per_layer : (l + 1) * per_layer]
            up_shift = rows[8:].reshape(ratio, n, width).transpose(1, 0, 2).reshape(1, -1)
            no_bias = jnp.zeros((1, model_dim), f32)
            vectors.append(
                dict(
                    gain=(rows[0:1], rows[1:2]),
                    shift=(rows[2:3], rows[3:4]),
                    qkv=jnp.concatenate([rows[4:5], no_bias, rows[5:6]], axis=1),
                    out=rows[6:7],
                    down=rows[7:8],
                    up=up_shift,
                )
            )

    saved = [[None] * LAYERS for _ in images]
    grads = {}
    vector_rows = [[None] * LAYERS for _ in images]
    outs, shapes = {}, {}
    for l in range(LAYERS):
        for w in WEIGHTS:
            key = w + str(l)
            if packed[l] and w != "down":
                outs[key] = packed_kinds[w]
                shapes[key] = [shaped((BLOCKS, tall + width, model_dim), bf16)]
                continue
            total = {"qkv": 3 * model_dim, "up": hidden_dim + model_dim, "down": model_dim}[w]
            total += SIDE if (w, l) == ("qkv", 0) else 0
            masks = ways(SCATTER, key)[0]
            table = span_table(masks[::-1] + [PARTNER]) if exact else tuple(range(BLOCKS))
            rows = (hidden_dim if w == "down" else model_dim) // BLOCKS
            outs[key] = ((0, total, table, 0, BLOCKS // 2, 0, not exact),)
            shapes[key] = [shaped((BLOCKS // 2, rows, total), bf16)] * 2

    def old_of(l, i):
        return [saved[i][l]["packed"]] if packed[l] and "packed" in saved[i][l] else []

    def gave(key, values, l, i):
        if packed[l] and len(values) == 1:
            saved[i][l]["packed"] = values[0]
            return
        grads[key] = values if key not in grads else [a + b for a, b in zip(grads[key], values)]

    def forward_one(l):
        if not vectors:
            read_vectors()
        v = vectors[l]
        for i in images:
            s = saved[i][l] = {}
            s["x"] = box["tok"][i] if l == 0 else saved[i][l - 1]["next"]
            s["normed"], s["qkv"], s["att"], s["lse"] = attn_fwd(
                plan.tie(who),
                s["x"],
                box["keep"][i],
                v["gain"][0],
                v["shift"][0],
                v["qkv"],
                weights["qkv" + str(l)],
            )
            plan.ended(s, "lse")

    def forward_two(l):
        v = vectors[l]
        for i in images:
            s = saved[i][l]
            s["mid"], s["normed_two"], s["hidden"], s["slope"] = mlp_up(
                plan.tie(who),
                s["x"],
                s["att"],
                v["out"],
                v["gain"][1],
                v["shift"][1],
                v["up"],
                weights["up" + str(l)],
            )
            plan.ended(s, "normed_two")

    def forward_three(l):
        for i in images:
            s = saved[i][l]
            s["next"] = mlp_down(
                plan.tie(who),
                s["mid"],
                s["hidden"],
                vectors[l]["down"],
                box["keep"][i],
                weights["down" + str(l)],
                l == LAYERS - 1,
            )
            plan.ended(s, "next")

    def back_one(l):
        for i in images:
            s = saved[i][l]
            if l == LAYERS - 1:
                s["grad"] = box["cot"][i].astype(f32) * box["keep"][i]
            else:
                s["grad"] = saved[i][l + 1]["d_x"]
            key = "down" + str(l)
            *values, s["low"], s["g_down"] = down_grad(
                plan.tie(who), s["grad"], s["hidden"], outs[key], shapes[key]
            )
            plan.ended(s, "low")
            gave(key, values, l, i)

    def back_two(l):
        for i in images:
            s = saved[i][l]
            key = "up" + str(l)
            *values, s["d_mid"], s["d_att"], g_up, g_gain, g_shift, g_out = mlp_back(
                plan.tie(who),
                s["grad"],
                s["low"],
                s["slope"],
                s["mid"],
                s["normed_two"],
                s["att"],
                vectors[l]["gain"][1],
                weights[key],
                weights["down" + str(l)],
                outs[key],
                shapes[key],
                old_of(l, i),
            )
            plan.ended(s, "d_mid")
            gave(key, values, l, i)
            up_rows = g_up.reshape(n, ratio, width).transpose(1, 0, 2).reshape(ratio, -1)
            blank = jnp.zeros_like(g_gain)
            vector_rows[i][l] = [blank, g_gain, blank, g_shift, blank, blank, g_out, s["g_down"]]
            vector_rows[i][l].append(up_rows)

    def back_three(l):
        for i in images:
            s = saved[i][l]
            others = None
            if l == 0:
                others = jnp.concatenate(sum(vector_rows[i], []), axis=0)
                others = jnp.pad(others, ((0, SIDE - others.shape[0]), (0, 0)))
            key = "qkv" + str(l)
            *values, s["d_x"], g_gain, g_shift, g_q, g_v = attn_back(
                plan.tie(who),
                s["d_att"],
                s["qkv"],
                s["lse"],
                box["keep"][i],
                s["normed"],
                s["x"],
                s["d_mid"],
                vectors[l]["gain"][0],
                weights[key],
                others,
                (0, 2, 4, 5),
                l == 0,
                outs[key],
                shapes[key],
                old_of(l, i),
            )
            plan.ended(s, "d_x")
            gave(key, values, l, i)
            rows = vector_rows[i][l]
            rows[0], rows[2], rows[4], rows[5] = g_gain, g_shift, g_q, g_v

    for l in range(LAYERS):
        steps = (forward_one, forward_two, forward_three, back_one, back_two, back_three)
        for at, step in enumerate(steps):
            plan.add(KERNELS + 10 * at + l, functools.partial(step, l))

    def start_back(name, key, l):
        whole = jnp.stack([saved[i][l][key] for i in images])
        box["mine" + name] = whole[:, :local_len]
        box[name] = exchange(plan.tie(whole[:, local_len:]), 1, n)

    def finish_back(name):
        box[name] = joined(box["mine" + name], plan.tie(box[name]))
        plan.ended(box, name)

    plan.add(OUTPUT, functools.partial(start_back, "out", "next", LAYERS - 1))
    plan.add(OUTPUT + ENDS, functools.partial(finish_back, "out"))
    plan.add(INPUT_GRAD, functools.partial(start_back, "dx", "d_x", 0))
    plan.add(INPUT_GRAD + ENDS, functools.partial(finish_back, "dx"))

    results = {}

    def take(key):
        return grads[key]

    def final(key, value):
        results[key] = value
        plan.ended(results, key)

    def start_scatter(l):
        whole = sum(saved[i][l]["packed"] for i in images[1:]) if len(images) > 1 else None
        whole = saved[0][l]["packed"] if whole is None else whole + saved[0][l]["packed"]
        whole = whole.reshape(-1, model_dim)
        got = lax.psum_scatter(whole, AXES, scatter_dimension=0, tiled=True).astype(f32)

        def wide(name):
            at, count = chunks[name]
            part = got[width * at : width * (at + count)]
            return part.reshape(count, width, model_dim).swapaxes(0, 1).reshape(width, -1)

        results["qkv" + str(l)] = wide("qkv")
        results["up" + str(l)] = jnp.concatenate([wide("up"), wide("out")], axis=1)

    for l in reversed(range(LAYERS)):
        if packed[l]:
            plan.add(SCATTERED + l, functools.partial(start_scatter, l))
        for w in ("down",) if packed[l] else ("down", "up", "qkv"):
            key = w + str(l)
            given = functools.partial(take, key)
            name = OUTWARD + number(w, l)
            masks = ways(SCATTER, key)[0]
            plan_scatter(plan, name, given, masks, me, n, functools.partial(final, key))

    plan.run(ORDER if plan.tied else plain_order(plan))

    g_qkv, g_up, g_down = ([results[w + str(l)] for l in range(LAYERS)] for w in WEIGHTS)
    vector_out = g_qkv[0][:, 3 * model_dim :].T

    def pick(at):
        return jnp.stack([vector_out[l * per_layer + at] for l in range(LAYERS)])

    return (
        box["out"],
        box["dx"].astype(f32),
        jnp.stack([pick(0), pick(1)], axis=1),
        jnp.stack([pick(2), pick(3)], axis=1),
        jnp.stack([g[:, : 3 * model_dim] for g in g_qkv]),
        jnp.stack([pick(4), pick(5)], axis=1),
        jnp.stack([g[:, hidden_dim:] for g in g_up]),
        pick(6),
        jnp.stack([g[:, :hidden_dim] for g in g_up]),
        jnp.concatenate([pick(8 + q) for q in range(ratio)], axis=1),
        jnp.stack(g_down),
        pick(7),
    )


GATHER = dict(
    up0=("abyx",),
    down0=("xaby",),
    qkv0=("byxa",),
)
SCATTER = dict(
    up0=("xbay",),
    down0=("yxba",),
    qkv0=("yxba",),
    down1=("byxa",),
)
PLACE = 10
PLACES = {}
ORDER = (
    2011, 0, 200, 400, 2000, 2001, 50, 1, 250, 201, 450, 401, 2050, 2051, 51, 2, 251, 202, 451,
    402, 52, 3, 252, 203, 452, 403, 53, 21, 20, 220, 253, 221, 453, 421, 71, 420, 70, 3000, 270,
    271, 3010, 471, 470, 3020, 3001, 3011, 3031, 1500, 3041, 3051, 2021, 3030, 1400, 3040, 1200,
    1550, 1501, 1450, 1401, 1250, 1201, 3050, 2003, 1000, 3021, 1551, 1502, 1451, 1402, 1251,
    1202, 2053, 1050, 1001, 1552, 1503, 2002, 1452, 1403, 1252, 1203, 1051, 1002, 1553, 1504,
    2052, 1453, 1404, 1253, 1204, 1052, 1003, 1554, 1454, 1254, 1053, 1004, 1054,
)


def solution(mesh):
    n_devices = mesh.shape["dp"] * mesh.shape["seq"]
    rows = P(None, AXES, None)
    last = P(None, None, AXES)
    flat = P(None, AXES)
    batch = P("dp", "seq", None)

    def body(*args):
        return per_device(n_devices, *args)

    return jax.shard_map(
        body,
        mesh=mesh,
        in_specs=(
            batch,
            P("dp", "seq"),
            last,
            last,
            rows,
            last,
            rows,
            flat,
            rows,
            flat,
            rows,
            flat,
            batch,
        ),
        out_specs=(batch, batch, last, last, rows, last, rows, flat, rows, flat, rows, flat),
        check_vma=False,
    )
```

```python
import functools

import jax
import jax.numpy as jnp
from jax import lax
from jax.experimental import pallas as pl
from jax.experimental.pallas import tpu as pltpu
from jax.sharding import PartitionSpec as P

HEAD = 64
BUFFER = 64
LAYERS = 2
AXES = ("dp", "seq")
BLOCKS = 32
SIDE = 128

masked_score = -1e30
f32 = jnp.float32
bf16 = jnp.bfloat16
INV_SQRT2 = 0.7071067811865476
INV_SQRT2PI = 0.3989422804014327

VMEM = pl.BlockSpec(memory_space=pltpu.VMEM)
SMEM = pl.BlockSpec(memory_space=pltpu.SMEM)
ANY = pl.BlockSpec(memory_space=pl.ANY)
weight_now = [10]
VMEM_LIMIT = 58 * 1024 * 1024


def mm(a, b):
    return lax.dot_general(a, b, (((1,), (0,)), ((), ())), preferred_element_type=f32)


def mm_nt(a, b):
    return lax.dot_general(a, b, (((1,), (1,)), ((), ())), preferred_element_type=f32)


def mm_tn(a, b):
    return lax.dot_general(a, b, (((0,), (0,)), ((), ())), preferred_element_type=f32)


def centred(x):
    mean = jnp.mean(x, axis=-1, keepdims=True)
    c = x - mean
    r = lax.rsqrt(jnp.mean(c * c, axis=-1, keepdims=True) + 1e-06)
    return c * r, r


def norm_back(d, n, r, gain):
    e = d * gain
    mean_e = jnp.mean(e, axis=-1, keepdims=True)
    mean_en = jnp.mean(e * n, axis=-1, keepdims=True)
    return r * (e - mean_e - n * mean_en)


def columns_sum(v):
    return jnp.sum(v, axis=0, keepdims=True)


def fetch(colors, parts, me, dst, sem, start=0):
    stop = start + dst.shape[1]
    for first, width, table, at, per, base, fixed in colors:
        low, high = max(start, first), min(stop, first + width)
        if low >= high:
            continue
        rows = dst.shape[0] // len(table)
        for p, offset in enumerate(table):
            owner = p if fixed else me ^ offset
            to_rows = pl.ds(pl.multiple_of(owner * rows, rows), rows)
            cols = pl.ds(low - first, high - low)
            src = parts[at + p // per].at[p % per, pl.ds(base, rows), cols]
            to = dst.at[to_rows, pl.ds(low - start, high - low)]
            pltpu.make_async_copy(src, to, sem).start()


def arrived(dst, sem):
    pltpu.make_async_copy(dst, dst, sem).wait()


def spread(src, out, me, arrays, sem, start):
    first, _, table, at, per, base, fixed = out
    width = src.shape[1]
    rows = src.shape[0] // len(table)
    for p, offset in enumerate(table):
        owner = p if fixed else me ^ offset
        from_rows = pl.ds(pl.multiple_of(owner * rows, rows), rows)
        to = arrays[at + p // per].at[p % per, pl.ds(base, rows), pl.ds(start, width)]
        pltpu.make_async_copy(src.at[from_rows, :], to, sem).start()


def holds(outs, column):
    return [o for o in outs if o[0] <= column < o[0] + o[1]][0]


def attn_fwd_body(colors, many, me_ref, x_ref, flag_ref, gain_ref, shift_ref, bias_ref, *refs):
    parts, refs = refs[:many], refs[many:]
    normed_ref, qkv_ref, att_ref, lse_ref, w, sem = refs
    dim = x_ref.shape[1]
    fetch(colors, parts, me_ref[0], w, sem)
    n, _ = centred(x_ref[...].astype(f32))
    normed_ref[...] = (n * gain_ref[...] + shift_ref[...]).astype(bf16)
    arrived(w, sem)

    def project(c, carry):
        cols = pl.ds(pl.multiple_of(c * 512, 512), 512)
        qkv_ref[:, cols] = (mm(normed_ref[...], w[:, cols]) + bias_ref[:, cols]).astype(bf16)
        return carry

    lax.fori_loop(0, 3 * dim // 512, project, 0)
    allowed = flag_ref[...] > 0
    scale = HEAD ** (-0.5)

    def two_heads(hp, carry):
        base = pl.multiple_of(hp * 128, 128)
        q2 = qkv_ref[:, pl.ds(base, 128)]
        k2 = qkv_ref[:, pl.ds(pl.multiple_of(dim + hp * 128, 128), 128)]
        v2 = qkv_ref[:, pl.ds(pl.multiple_of(2 * dim + hp * 128, 128), 128)]
        outs = []
        for s in range(2):
            cut = slice(s * HEAD, (s + 1) * HEAD)
            score = jnp.where(allowed, mm_nt(k2[:, cut], q2[:, cut]) * scale, masked_score)
            top = jnp.max(score, axis=0, keepdims=True)
            e = jnp.exp(score - top)
            total = jnp.sum(e, axis=0, keepdims=True)
            probs = (e * (1.0 / total)).astype(bf16)
            lse_ref[pl.ds(2 * hp + s, 1), :] = top + jnp.log(total)
            outs.append(mm_tn(probs, v2[:, cut]))
        att_ref[:, pl.ds(base, 128)] = jnp.concatenate(outs, axis=1).astype(bf16)
        return carry

    lax.fori_loop(0, dim // 128, two_heads, 0)


def mlp_up_body(colors, many, me_ref, x_ref, att_ref, ob_ref, gain_ref, shift_ref, ub_ref, *refs):
    parts, refs = refs[:many], refs[many:]
    mid_ref, normed_ref, hidden_ref, slope_ref, w_out, w_up, sem = refs
    ff = ub_ref.shape[1]
    fetch(colors, parts, me_ref[0], w_out, sem.at[0], ff)
    fetch(colors, parts, me_ref[0], w_up, sem.at[1])
    arrived(w_out, sem.at[0])
    mid = x_ref[...].astype(f32) + mm(att_ref[...], w_out[...]) + ob_ref[...]
    mid_ref[...] = mid
    n, _ = centred(mid)
    normed_ref[...] = (n * gain_ref[...] + shift_ref[...]).astype(bf16)
    arrived(w_up, sem.at[1])

    def step(c, carry):
        cols = pl.ds(pl.multiple_of(c * 512, 512), 512)
        u = mm(normed_ref[...], w_up[:, cols]) + ub_ref[:, cols]
        phi = 0.5 + 0.5 * lax.erf(u * INV_SQRT2)
        hidden_ref[:, cols] = (u * phi).astype(bf16)
        slope_ref[:, cols] = phi + u * (INV_SQRT2PI * jnp.exp(-0.5 * u * u))
        return carry

    lax.fori_loop(0, ff // 512, step, 0)


def mlp_down_body(colors, many, last, me_ref, mid_ref, hidden_ref, db_ref, flag_ref, *refs):
    parts, refs = refs[:many], refs[many:]
    out_ref, w, sem = refs
    fetch(colors, parts, me_ref[0], w, sem)
    arrived(w, sem)
    for c in range(0, w.shape[1], 512):
        cols = slice(c, c + 512)
        y = mid_ref[:, cols] + mm(hidden_ref[...], w[:, cols]) + db_ref[:, cols]
        if last:
            y = (y * flag_ref[...]).astype(bf16)
        out_ref[:, cols] = y


def down_grad_body(outs, many, me_ref, grad_ref, hidden_ref, *refs):
    arrays, refs = refs[:many], refs[many:]
    low_ref, sum_ref, perm, tile, sem = refs
    me = me_ref[0]
    grad = grad_ref[...]
    low_ref[...] = grad.astype(bf16)
    sum_ref[...] = columns_sum(grad)
    group = 4
    ((first, width, table, at, per, base, fixed),) = outs
    rows = hidden_ref.shape[1] // len(table)
    for p, offset in enumerate(table):
        owner = pl.ds(pl.multiple_of((p if fixed else me ^ offset) * rows, rows), rows)
        perm[:, p * rows : (p + 1) * rows] = hidden_ref[:, owner]
    pending = [None, None]
    for g in reversed(range(len(table) // group)):
        slot = g % 2
        if pending[slot] is not None:
            pending[slot].wait()
        cut = slice(g * group * rows, (g + 1) * group * rows)
        block = mm_tn(perm[:, cut], low_ref[...])
        tile[slot] = block.astype(bf16).reshape(tile.shape[1:])
        b0 = g * group
        to = arrays[at + b0 // per].at[pl.ds(b0 % per, group), pl.ds(base, rows)]
        pending[slot] = pltpu.make_async_copy(tile.at[slot], to, sem.at[slot])
        pending[slot].start()
    for copy in pending:
        copy.wait()


def mlp_back_body(ups, downs, outs, many, me_ref, grad_ref, low_ref, slope_ref, mid_ref, *refs):
    normed_ref, att_ref, gain_ref, refs = refs[0], refs[1], refs[2], refs[3:]
    many_up, many_down, many_in, many_out = many
    up_parts, refs = refs[:many_up], refs[many_up:]
    down_parts, refs = refs[:many_down], refs[many_down:]
    refs = refs[many_in:]
    halves, refs = refs[:many_out], refs[many_out:]
    d_mid_ref, d_att_ref, g_up_ref, g_gain, g_shift, g_out, refs = (*refs[:6], refs[6:])
    w_down, w_up, w_out, turned, turned_att, d_low_ref, acc, tile, low_mid, sem, out_sem = refs
    me = me_ref[0]
    ff, dim = w_down.shape
    fetch(downs, down_parts, me, w_down, sem.at[0])
    fetch(ups, up_parts, me, w_up, sem.at[1])
    fetch(ups, up_parts, me, w_out, sem.at[2], ff)
    turned[...] = normed_ref[...].T
    turned_att[...] = att_ref[...].T
    acc[...] = jnp.zeros_like(acc)
    arrived(w_down, sem.at[0])

    def first_step(c, carry):
        cols = pl.ds(pl.multiple_of(c * 512, 512), 512)
        d_up = mm_nt(low_ref[...], w_down[cols, :]) * slope_ref[:, cols]
        g_up_ref[:, cols] = columns_sum(d_up)
        d_low_ref[:, cols] = d_up.astype(bf16)
        return carry

    lax.fori_loop(0, ff // 512, first_step, 0)
    arrived(w_up, sem.at[1])

    def flush(slot):
        pltpu.make_async_copy(tile.at[slot], tile.at[slot], out_sem.at[slot]).wait()

    for out in outs:
        first, width = out[:2]
        stop = min(first + width, ff)

        def step(c, carry, out=out, first=first):
            start = pl.multiple_of(c * 512, 512)
            cols = pl.ds(start, 512)
            slot = lax.rem(c, 2)

            @pl.when(c >= 2)
            def _():
                flush(slot)

            tile[slot] = mm(turned[...], d_low_ref[:, cols]).astype(bf16)
            local = pl.multiple_of(start - first, 512)
            spread(tile.at[slot], out, me, halves, out_sem.at[slot], local)
            acc[...] += mm_nt(d_low_ref[:, cols], w_up[:, cols])
            return carry

        lax.fori_loop(first // 512, stop // 512, step, 0)
    n, r = centred(mid_ref[...])
    d = acc[...]
    g_gain[...] = columns_sum(d * n)
    g_shift[...] = columns_sum(d)
    d_mid = grad_ref[...] + norm_back(d, n, r, gain_ref[...])
    d_mid_ref[...] = d_mid
    g_out[...] = columns_sum(d_mid)
    low_mid[...] = d_mid.astype(bf16)
    arrived(w_out, sem.at[2])
    for c in range(dim // 512):
        flush(c % 2)
        tile[c % 2] = mm(turned_att[...], low_mid[:, c * 512 : (c + 1) * 512]).astype(bf16)
        start = ff + c * 512
        out = holds(outs, start)
        spread(tile.at[c % 2], out, me, halves, out_sem.at[c % 2], start - out[0])
    d_att_ref[...] = mm_nt(low_mid[...], w_out[...]).astype(bf16)
    flush(0)
    flush(1)


def attn_back_body(colors, outs, counts, extra, me_ref, d_att_ref, qkv_ref, lse_ref, flag_ref, *refs):
    many, many_in, many_out = counts
    normed_ref, x_ref, d_mid_ref, gain_ref, refs = *refs[:4], refs[4:]
    if extra:
        others_ref, refs = refs[0], refs[1:]
    parts, refs = refs[:many], refs[many:]
    refs = refs[many_in:]
    halves, refs = refs[:many_out], refs[many_out:]
    d_x_ref, g_gain, g_shift, g_query, g_value, refs = (*refs[:5], refs[5:])
    if extra:
        w, d_qkv, turned, tile, sem, out_sem, column, wide = refs
    else:
        w, d_qkv, turned, tile, sem, out_sem = refs
    me = me_ref[0]
    dim = x_ref.shape[1]
    fetch(colors, parts, me, w, sem)
    turned[...] = normed_ref[...].T
    allowed = flag_ref[...] > 0
    scale = HEAD ** (-0.5)

    def two_heads(hp, carry):
        at_q = pl.ds(pl.multiple_of(hp * 128, 128), 128)
        at_k = pl.ds(pl.multiple_of(dim + hp * 128, 128), 128)
        at_v = pl.ds(pl.multiple_of(2 * dim + hp * 128, 128), 128)
        q2, k2, v2, d2 = qkv_ref[:, at_q], qkv_ref[:, at_k], qkv_ref[:, at_v], d_att_ref[:, at_q]
        dq, dk, dv = [], [], []
        for s in range(2):
            cut = slice(s * HEAD, (s + 1) * HEAD)
            q, k, v, d = q2[:, cut], k2[:, cut], v2[:, cut], d2[:, cut]
            score = jnp.where(allowed, mm_nt(k, q) * scale, masked_score)
            probs = jnp.exp(score - lse_ref[pl.ds(2 * hp + s, 1), :])
            dv.append(mm(probs.astype(bf16), d))
            d_probs = mm_nt(v, d)
            inner = jnp.sum(probs * d_probs, axis=0, keepdims=True)
            d_score = (probs * (d_probs - inner)).astype(bf16)
            dq.append(mm_tn(d_score, k) * scale)
            dk.append(mm(d_score, q) * scale)
        d_qkv[:, at_q] = jnp.concatenate(dq, axis=1).astype(bf16)
        d_qkv[:, at_k] = jnp.concatenate(dk, axis=1).astype(bf16)
        d_qkv[:, at_v] = jnp.concatenate(dv, axis=1).astype(bf16)
        return carry

    lax.fori_loop(0, dim // 128, two_heads, 0)

    def flush(slot):
        pltpu.make_async_copy(tile.at[slot], tile.at[slot], out_sem.at[slot]).wait()

    for c in range(3 * dim // 512):
        if c >= 2:
            flush(c % 2)
        tile[c % 2] = mm(turned[...], d_qkv[:, c * 512 : (c + 1) * 512]).astype(bf16)
        out = holds(outs, c * 512)
        spread(tile.at[c % 2], out, me, halves, out_sem.at[c % 2], c * 512 - out[0])
    g_query[...] = columns_sum(d_qkv[:, :dim].astype(f32))
    g_value[...] = columns_sum(d_qkv[:, 2 * dim :].astype(f32))
    arrived(w, sem)
    d = mm_nt(d_qkv[...], w[...])
    n, r = centred(x_ref[...].astype(f32))
    g_gain[...] = columns_sum(d * n)
    g_shift[...] = columns_sum(d)
    d_x_ref[...] = (d_mid_ref[...] + norm_back(d, n, r, gain_ref[...])).astype(d_x_ref.dtype)
    if extra:
        wide[...] = others_ref[...]
        for at, row in zip(extra, (g_gain, g_shift, g_query, g_value)):
            wide[at : at + 1, :] = row[...]
        column[...] = wide[...].T.astype(bf16)
        spread(column, outs[-1], me, halves, sem, 3 * dim - outs[-1][0])
        arrived(column, sem)
    flush(0)
    flush(1)


def shaped(shape, dtype=f32):
    return jax.ShapeDtypeStruct(shape, dtype)


def call(body, name, in_specs, out_shapes, out_specs, scratch, args, aliases=None):
    return pl.pallas_call(
        body,
        in_specs=in_specs,
        out_specs=out_specs,
        out_shape=out_shapes,
        scratch_shapes=scratch,
        input_output_aliases=aliases or {},
        compiler_params=pltpu.CompilerParams(vmem_limit_bytes=VMEM_LIMIT),
        cost_estimate=pl.CostEstimate(
            flops=10 ** weight_now[0], bytes_accessed=0, transcendentals=0
        ),
        name=name,
    )(*args)


def attn_fwd(me, x, flag, gain, shift, bias, weight):
    length, dim = x.shape
    colors, parts = weight
    return call(
        functools.partial(attn_fwd_body, colors, len(parts)),
        "attn_fwd",
        [SMEM] + [VMEM] * 5 + [ANY] * len(parts),
        (
            shaped((length, dim), bf16),
            shaped((length, 3 * dim), bf16),
            shaped((length, dim), bf16),
            shaped((dim // HEAD, length)),
        ),
        (VMEM,) * 4,
        [pltpu.VMEM((dim, 3 * dim), bf16), pltpu.SemaphoreType.DMA],
        (me, x, flag, gain, shift, bias, *parts),
    )


def mlp_up(me, x, att, out_bias, gain, shift, up_bias, weight):
    length, dim = x.shape
    ff = up_bias.shape[1]
    colors, parts = weight
    return call(
        functools.partial(mlp_up_body, colors, len(parts)),
        "mlp_up",
        [SMEM] + [VMEM] * 6 + [ANY] * len(parts),
        (
            shaped((length, dim)),
            shaped((length, dim), bf16),
            shaped((length, ff), bf16),
            shaped((length, ff)),
        ),
        (VMEM,) * 4,
        [
            pltpu.VMEM((dim, dim), bf16),
            pltpu.VMEM((dim, ff), bf16),
            pltpu.SemaphoreType.DMA((2,)),
        ],
        (me, x, att, out_bias, gain, shift, up_bias, *parts),
    )


def mlp_down(me, mid, hidden, down_bias, flag, weight, last):
    length, dim = mid.shape
    ff = hidden.shape[1]
    colors, parts = weight
    return call(
        functools.partial(mlp_down_body, colors, len(parts), last),
        "mlp_down",
        [SMEM] + [VMEM] * 4 + [ANY] * len(parts),
        shaped((length, dim), bf16 if last else f32),
        VMEM,
        [pltpu.VMEM((ff, dim), bf16), pltpu.SemaphoreType.DMA],
        (me, mid, hidden, down_bias, flag, *parts),
    )


def down_grad(me, grad, hidden, outs, shapes):
    length, dim = grad.shape
    ff = hidden.shape[1]
    return call(
        functools.partial(down_grad_body, outs, len(shapes)),
        "down_grad",
        [SMEM, VMEM, VMEM],
        (*shapes, shaped((length, dim), bf16), shaped((1, dim))),
        (ANY,) * len(shapes) + (VMEM, VMEM),
        [
            pltpu.VMEM((length, ff), bf16),
            pltpu.VMEM((2, 4, ff // BLOCKS, dim), bf16),
            pltpu.SemaphoreType.DMA((2,)),
        ],
        (me, grad, hidden),
    )


def mlp_back(me, grad, low, slope, mid, normed, att, gain, up_weight, down_weight, outs, shapes, old):
    length, dim = grad.shape
    ff = slope.shape[1]
    ups, up_parts = up_weight
    downs, down_parts = down_weight
    many = (len(up_parts), len(down_parts), len(old), len(shapes))
    row = shaped((1, dim))
    return call(
        functools.partial(mlp_back_body, ups, downs, outs, many),
        "mlp_back",
        [SMEM] + [VMEM] * 7 + [ANY] * (len(up_parts) + len(down_parts) + len(old)),
        (
            *shapes,
            shaped((length, dim)),
            shaped((length, dim), bf16),
            shaped((1, ff)),
            row,
            row,
            row,
        ),
        (ANY,) * len(shapes) + (VMEM,) * 6,
        [
            pltpu.VMEM((ff, dim), bf16),
            pltpu.VMEM((dim, ff), bf16),
            pltpu.VMEM((dim, dim), bf16),
            pltpu.VMEM((dim, length), bf16),
            pltpu.VMEM((dim, length), bf16),
            pltpu.VMEM((length, ff), bf16),
            pltpu.VMEM((length, dim), f32),
            pltpu.VMEM((2, dim, 512), bf16),
            pltpu.VMEM((length, dim), bf16),
            pltpu.SemaphoreType.DMA((3,)),
            pltpu.SemaphoreType.DMA((2,)),
        ],
        (me, grad, low, slope, mid, normed, att, gain, *up_parts, *down_parts, *old),
        {8 + len(up_parts) + len(down_parts): 0} if old else None,
    )


def attn_back(me, d_att, qkv, lse, flag, normed, x, d_mid, gain, weight, others, at, last, outs, shapes, old):
    length, dim = x.shape
    colors, parts = weight
    extra = () if others is None else tuple(at)
    counts = (len(parts), len(old), len(shapes))
    before = 10 if extra else 9
    row = shaped((1, dim))
    scratch = [
        pltpu.VMEM((dim, 3 * dim), bf16),
        pltpu.VMEM((length, 3 * dim), bf16),
        pltpu.VMEM((dim, length), bf16),
        pltpu.VMEM((2, dim, 512), bf16),
        pltpu.SemaphoreType.DMA,
        pltpu.SemaphoreType.DMA((2,)),
    ]
    if extra:
        scratch += [pltpu.VMEM((dim, SIDE), bf16), pltpu.VMEM((SIDE, dim), f32)]
    return call(
        functools.partial(attn_back_body, colors, outs, counts, extra),
        "attn_back",
        [SMEM] + [VMEM] * (before - 1) + [ANY] * (len(parts) + len(old)),
        (*shapes, shaped((length, dim), bf16 if last else f32), row, row, row, row),
        (ANY,) * len(shapes) + (VMEM,) * 5,
        scratch,
        (me, d_att, qkv, lse, flag, normed, x, d_mid, gain)
        + ((others,) if extra else ())
        + tuple(parts)
        + tuple(old),
        {before + len(parts): 0} if old else None,
    )


def pack_body(a_ref, b_ref, out_ref):
    half = a_ref.shape[0]

    def step(i, carry):
        out_ref[i] = a_ref[i]
        out_ref[half + i] = b_ref[i]
        return carry

    lax.fori_loop(0, half, step, 0)


def pack(a, b):
    shape = (a.shape[0] * 2, *a.shape[1:])
    return call(pack_body, "pack", [VMEM] * 2, shaped(shape, bf16), VMEM, [], (a, b))


def merge_body(keep_ref, got_ref, low_ref, high_ref):
    half = low_ref.shape[0]

    def step(i, carry):
        low_ref[i] = keep_ref[i] + got_ref[i]
        high_ref[i] = keep_ref[half + i] + got_ref[half + i]
        return carry

    lax.fori_loop(0, half, step, 0)


def merge(keep, got):
    half = shaped((keep.shape[0] // 2, *keep.shape[1:]), bf16)
    return call(
        merge_body, "merge", [VMEM] * 2, (half, half), (VMEM, VMEM), [], (keep, got)
    )


def exchange(value, mask, n):
    return lax.ppermute(value, AXES, [(i, i ^ mask) for i in range(n)])


PARTNER = 2
NAMED = dict(x=1, y=4, b=8, a=24)


def other_masks(n):
    bits = n.bit_length() - 1
    return [1 << k for k in range(bits - 1, 1, -1)] + [1]


def span_table(masks):
    table = [0]
    for m in masks:
        table = table + [t ^ m for t in table]
    return tuple(table)


def owners_of(masks, me):
    return me ^ jnp.asarray(span_table(masks), jnp.int32)


def positions_of(masks, me):
    table = span_table(masks)
    inverse = [0] * len(table)
    for p, t in enumerate(table):
        inverse[t] = p
    return jnp.asarray(inverse, jnp.int32)[me ^ jnp.arange(len(table), dtype=jnp.int32)]


class Plan:
    def __init__(self, tied):
        self.actions = {}
        self.tied = tied
        self.last = None

    def ended(self, holder, key):
        self.last = (holder, key)

    def tie(self, value):
        if not self.tied or self.last is None:
            return value
        holder, key = self.last
        value, holder[key] = lax.optimization_barrier((value, holder[key]))
        return value

    def add(self, name, action):
        self.actions[name] = action

    def run(self, order):
        left = dict(self.actions)
        for name in order:
            weight_now[0] = PLACES.get(name, PLACE)
            left.pop(name)()
        assert not left, sorted(left)


def plan_gather(plan, name, own, masks, me, n, ready):
    state = dict(held=own[None])
    last = len(masks) - 1

    def start(k):
        state["got"] = exchange(plan.tie(state["held"]), masks[k], n)

    def finish(k):
        got = plan.tie(state["got"])
        if k < last:
            state["held"] = pack(state["held"], got)
            plan.ended(state, "held")
        else:
            state["end"] = got
            plan.ended(state, "end")

    def cross(k):
        state[k] = exchange(plan.tie(state["held" if k == 1 else "end"]), PARTNER, n)

    def crossed(k):
        state[k] = plan.tie(state[k])
        plan.ended(state, k)
        if k == 2:
            whole = masks + [PARTNER]
            parts = [state["held"], state["end"], state[1], state[2]]
            if n == BLOCKS:
                ready(span_table(whole), parts)
                plan.ended(parts, 3)
            else:
                joined = jnp.concatenate(parts, axis=0)[positions_of(whole, me)]
                joined = joined.reshape(4, BLOCKS // 4, -1, own.shape[1])
                ready(tuple(range(BLOCKS)), list(joined))

    for k in range(len(masks)):
        plan.add(name + k, functools.partial(start, k))
        plan.add(name + k + ENDS, functools.partial(finish, k))
    for k in (1, 2):
        plan.add(name + 19 + k, functools.partial(cross, k))
        plan.add(name + 19 + k + ENDS, functools.partial(crossed, k))


def plan_scatter(plan, name, given, masks, me, n, ready):
    state = {}

    def start(k):
        if k < 0:
            keep, send = given()
            if n != BLOCKS:
                whole = jnp.concatenate([keep, send], axis=0).reshape(n, -1, keep.shape[2])
                whole = whole[owners_of(masks[::-1] + [PARTNER], me)]
                keep, send = whole[: n // 2], whole[n // 2 :]
            state["keep"], state["send"] = keep, send
        mask = PARTNER if k < 0 else masks[k]
        state["got"] = exchange(plan.tie(state["send"]), mask, n)

    def finish(k):
        keep, got = state["keep"], plan.tie(state["got"])
        if k == len(masks) - 1:
            ready((keep.astype(f32) + got.astype(f32))[0])
            return
        state["keep"], state["send"] = merge(keep, got)
        plan.ended(state, "keep")

    for k in range(-1, len(masks)):
        plan.add(name + k + 1, functools.partial(start, k))
        plan.add(name + k + 1 + ENDS, functools.partial(finish, k))


WEIGHTS = ("qkv", "up", "down")
ENDS = 50
OUTWARD = 1000
TOKENS, COTANGENT, OUTPUT, INPUT_GRAD = 2000, 2001, 2002, 2003
GATHERED, SCATTERED = 2010, 2020
KERNELS = 3000


def number(w, l):
    return 100 * (2 * WEIGHTS.index(w) + l)


def plain_order(plan):
    def stage(a):
        if a >= KERNELS:
            return (1, LAYERS * (a - KERNELS >= 30), -(a % 10) if a >= KERNELS + 30 else a % 10, a)
        late = OUTWARD <= a < TOKENS or a % ENDS >= 2 and a >= TOKENS
        return (2 if late else 0, 0, 0, 0)

    return sorted(plan.actions, key=stage)


def per_device(
    n_devices,
    tokens,
    keep,
    norm_gain,
    norm_bias,
    qkv_weight,
    qv_bias,
    out_weight,
    out_bias,
    up_weight,
    up_bias,
    down_weight,
    down_bias,
    cotangent,
):
    n = n_devices
    seq_at = lax.axis_index("seq")
    me = lax.axis_index("dp") * 2 + seq_at
    n_images, local_len, model_dim = tokens.shape
    half_images = n_images // 2
    width = norm_gain.shape[2]
    ratio = up_bias.shape[1] // width
    hidden_dim = up_bias.shape[1] * n
    exact = n == BLOCKS
    who = (me if exact else jnp.zeros_like(me)).reshape(1)
    images = range(half_images)
    plan = Plan(exact and half_images == 1)

    positions = seq_at * local_len + lax.iota(jnp.int32, local_len)
    key_keep = ((keep == 1) | (positions < BUFFER)[None, :]).astype(bf16)

    def halves(value):
        low, high = value[:half_images], value[half_images:]
        mine = jnp.where(seq_at == 0, low, high)
        other = jnp.where(seq_at == 0, high, low)
        return mine, other

    def joined(mine, other):
        return jnp.where(
            seq_at == 0,
            jnp.concatenate([mine, other], axis=0),
            jnp.concatenate([other, mine], axis=0),
        )

    tok_mine, tok_other = halves(tokens)
    cot_mine, cot_other = halves(cotangent)
    keep_mine, keep_other = halves(key_keep)
    box = {}

    def start_tokens():
        below = ((0, 0), (0, 7), (0, model_dim - local_len))
        flags = jnp.pad(keep_other[:, None, :], below)
        sent = jnp.concatenate([tok_other, flags], axis=1)
        box["sent"] = exchange(plan.tie(sent), 1, n)

    def finish_tokens():
        got = plan.tie(box["sent"])
        box["tok"] = jnp.concatenate([tok_mine, got[:, :local_len]], axis=1)
        flags = jnp.concatenate([keep_mine, got[:, local_len, :local_len]], axis=1)
        box["keep"] = flags.astype(f32)[:, :, None]
        plan.ended(box, "tok")

    def start_cotangent():
        box["cot"] = exchange(plan.tie(cot_other), 1, n)

    def finish_cotangent():
        box["cot"] = jnp.concatenate([cot_mine, plan.tie(box["cot"])], axis=1)
        plan.ended(box, "cot")

    plan.add(TOKENS, start_tokens)
    plan.add(TOKENS + ENDS, finish_tokens)
    plan.add(COTANGENT, start_cotangent)
    plan.add(COTANGENT + ENDS, finish_cotangent)

    def columns(l):
        return [norm_gain[l, 0], norm_gain[l, 1], norm_bias[l, 0], norm_bias[l, 1]] + [
            qv_bias[l, 0],
            qv_bias[l, 1],
            out_bias[l],
            down_bias[l],
        ] + [up_bias[l, q * width : (q + 1) * width] for q in range(ratio)]

    stacked = jnp.stack(sum([columns(l) for l in range(LAYERS)], []))
    per_layer = stacked.shape[0] // LAYERS
    stacked = jnp.pad(stacked, ((0, SIDE - stacked.shape[0]), (0, 0))).T

    def ways(table, key):
        return [[NAMED[c] for c in way] for way in table[key]] if exact else [other_masks(n)]

    weights = {}
    packed = [exact and l == LAYERS - 1 for l in range(LAYERS)]
    chunks = dict(qkv=(0, 3), out=(3, 1), up=(4, ratio))
    tall = width * (4 + ratio)

    def receive(key, size, table, parts):
        weights[key] = (((0, size, table, 0, parts[0].shape[0], 0, not exact),), parts)

    def packed_colors(name, start=0):
        at, count = chunks[name]
        same = tuple(range(BLOCKS))
        return tuple(
            (start + c * model_dim, model_dim, same, 0, BLOCKS, width * (at + c), True)
            for c in range(count)
        )

    packed_kinds = dict(
        qkv=packed_colors("qkv"),
        up=packed_colors("up") + packed_colors("out", hidden_dim),
        down=((0, model_dim, tuple(range(BLOCKS)), 0, BLOCKS, tall, True),),
    )

    def start_packed(l):
        def rows(value):
            return value.reshape(width, -1, model_dim).swapaxes(0, 1).reshape(-1, model_dim)

        own = [rows(qkv_weight[l]), out_weight[l], rows(up_weight[l]), down_weight[l]]
        own = plan.tie(jnp.concatenate(own, axis=0))
        whole = lax.all_gather(own, AXES, axis=0, tiled=False)
        for w in WEIGHTS:
            weights[w + str(l)] = (packed_kinds[w], [whole])

    for l in range(LAYERS):
        if packed[l]:
            plan.add(GATHERED + l, functools.partial(start_packed, l))
            continue
        for w in WEIGHTS:
            key = w + str(l)
            if w == "qkv":
                own = qkv_weight[l]
                if l == 0:
                    own = jnp.concatenate([own, stacked], axis=1)
            elif w == "up":
                own = jnp.concatenate([up_weight[l], out_weight[l]], axis=1)
            else:
                own = down_weight[l]
            masks = ways(GATHER, key)[0]
            got = functools.partial(receive, key, own.shape[1])
            plan_gather(plan, number(w, l), own, masks, me, n, got)

    vectors = []

    def read_vectors():
        parts = weights["qkv0"][1]
        side = jnp.concatenate([part[:, :, 3 * model_dim :] for part in parts], axis=0)
        if exact:
            side = side[positions_of(ways(GATHER, "qkv0")[0] + [PARTNER], me)]
        side = side.reshape(model_dim, SIDE).T.astype(f32)
        for l in range(LAYERS):
            rows = side[l * per_layer : (l + 1) * per_layer]
            up_shift = rows[8:].reshape(ratio, n, width).transpose(1, 0, 2).reshape(1, -1)
            no_bias = jnp.zeros((1, model_dim), f32)
            vectors.append(
                dict(
                    gain=(rows[0:1], rows[1:2]),
                    shift=(rows[2:3], rows[3:4]),
                    qkv=jnp.concatenate([rows[4:5], no_bias, rows[5:6]], axis=1),
                    out=rows[6:7],
                    down=rows[7:8],
                    up=up_shift,
                )
            )

    saved = [[None] * LAYERS for _ in images]
    grads = {}
    vector_rows = [[None] * LAYERS for _ in images]
    outs, shapes = {}, {}
    for l in range(LAYERS):
        for w in WEIGHTS:
            key = w + str(l)
            if packed[l] and w != "down":
                outs[key] = packed_kinds[w]
                shapes[key] = [shaped((BLOCKS, tall + width, model_dim), bf16)]
                continue
            total = {"qkv": 3 * model_dim, "up": hidden_dim + model_dim, "down": model_dim}[w]
            total += SIDE if (w, l) == ("qkv", 0) else 0
            masks = ways(SCATTER, key)[0]
            table = span_table(masks[::-1] + [PARTNER]) if exact else tuple(range(BLOCKS))
            rows = (hidden_dim if w == "down" else model_dim) // BLOCKS
            outs[key] = ((0, total, table, 0, BLOCKS // 2, 0, not exact),)
            shapes[key] = [shaped((BLOCKS // 2, rows, total), bf16)] * 2

    def old_of(l, i):
        return [saved[i][l]["packed"]] if packed[l] and "packed" in saved[i][l] else []

    def gave(key, values, l, i):
        if packed[l] and len(values) == 1:
            saved[i][l]["packed"] = values[0]
            return
        grads[key] = values if key not in grads else [a + b for a, b in zip(grads[key], values)]

    def forward_one(l):
        if not vectors:
            read_vectors()
        v = vectors[l]
        for i in images:
            s = saved[i][l] = {}
            s["x"] = box["tok"][i] if l == 0 else saved[i][l - 1]["next"]
            s["normed"], s["qkv"], s["att"], s["lse"] = attn_fwd(
                plan.tie(who),
                s["x"],
                box["keep"][i],
                v["gain"][0],
                v["shift"][0],
                v["qkv"],
                weights["qkv" + str(l)],
            )
            plan.ended(s, "lse")

    def forward_two(l):
        v = vectors[l]
        for i in images:
            s = saved[i][l]
            s["mid"], s["normed_two"], s["hidden"], s["slope"] = mlp_up(
                plan.tie(who),
                s["x"],
                s["att"],
                v["out"],
                v["gain"][1],
                v["shift"][1],
                v["up"],
                weights["up" + str(l)],
            )
            plan.ended(s, "normed_two")

    def forward_three(l):
        for i in images:
            s = saved[i][l]
            s["next"] = mlp_down(
                plan.tie(who),
                s["mid"],
                s["hidden"],
                vectors[l]["down"],
                box["keep"][i],
                weights["down" + str(l)],
                l == LAYERS - 1,
            )
            plan.ended(s, "next")

    def back_one(l):
        for i in images:
            s = saved[i][l]
            if l == LAYERS - 1:
                s["grad"] = box["cot"][i].astype(f32) * box["keep"][i]
            else:
                s["grad"] = saved[i][l + 1]["d_x"]
            key = "down" + str(l)
            *values, s["low"], s["g_down"] = down_grad(
                plan.tie(who), s["grad"], s["hidden"], outs[key], shapes[key]
            )
            plan.ended(s, "low")
            gave(key, values, l, i)

    def back_two(l):
        for i in images:
            s = saved[i][l]
            key = "up" + str(l)
            *values, s["d_mid"], s["d_att"], g_up, g_gain, g_shift, g_out = mlp_back(
                plan.tie(who),
                s["grad"],
                s["low"],
                s["slope"],
                s["mid"],
                s["normed_two"],
                s["att"],
                vectors[l]["gain"][1],
                weights[key],
                weights["down" + str(l)],
                outs[key],
                shapes[key],
                old_of(l, i),
            )
            plan.ended(s, "d_mid")
            gave(key, values, l, i)
            up_rows = g_up.reshape(n, ratio, width).transpose(1, 0, 2).reshape(ratio, -1)
            blank = jnp.zeros_like(g_gain)
            vector_rows[i][l] = [blank, g_gain, blank, g_shift, blank, blank, g_out, s["g_down"]]
            vector_rows[i][l].append(up_rows)

    def back_three(l):
        for i in images:
            s = saved[i][l]
            others = None
            if l == 0:
                others = jnp.concatenate(sum(vector_rows[i], []), axis=0)
                others = jnp.pad(others, ((0, SIDE - others.shape[0]), (0, 0)))
            key = "qkv" + str(l)
            *values, s["d_x"], g_gain, g_shift, g_q, g_v = attn_back(
                plan.tie(who),
                s["d_att"],
                s["qkv"],
                s["lse"],
                box["keep"][i],
                s["normed"],
                s["x"],
                s["d_mid"],
                vectors[l]["gain"][0],
                weights[key],
                others,
                (0, 2, 4, 5),
                l == 0,
                outs[key],
                shapes[key],
                old_of(l, i),
            )
            plan.ended(s, "d_x")
            gave(key, values, l, i)
            rows = vector_rows[i][l]
            rows[0], rows[2], rows[4], rows[5] = g_gain, g_shift, g_q, g_v

    for l in range(LAYERS):
        steps = (forward_one, forward_two, forward_three, back_one, back_two, back_three)
        for at, step in enumerate(steps):
            plan.add(KERNELS + 10 * at + l, functools.partial(step, l))

    def start_back(name, key, l):
        whole = jnp.stack([saved[i][l][key] for i in images])
        box["mine" + name] = whole[:, :local_len]
        box[name] = exchange(plan.tie(whole[:, local_len:]), 1, n)

    def finish_back(name):
        box[name] = joined(box["mine" + name], plan.tie(box[name]))
        plan.ended(box, name)

    plan.add(OUTPUT, functools.partial(start_back, "out", "next", LAYERS - 1))
    plan.add(OUTPUT + ENDS, functools.partial(finish_back, "out"))
    plan.add(INPUT_GRAD, functools.partial(start_back, "dx", "d_x", 0))
    plan.add(INPUT_GRAD + ENDS, functools.partial(finish_back, "dx"))

    results = {}

    def take(key):
        return grads[key]

    def final(key, value):
        results[key] = value
        plan.ended(results, key)

    def start_scatter(l):
        whole = sum(saved[i][l]["packed"] for i in images[1:]) if len(images) > 1 else None
        whole = saved[0][l]["packed"] if whole is None else whole + saved[0][l]["packed"]
        whole = whole.reshape(-1, model_dim)
        got = lax.psum_scatter(whole, AXES, scatter_dimension=0, tiled=True).astype(f32)

        def wide(name):
            at, count = chunks[name]
            part = got[width * at : width * (at + count)]
            return part.reshape(count, width, model_dim).swapaxes(0, 1).reshape(width, -1)

        results["qkv" + str(l)] = wide("qkv")
        results["up" + str(l)] = jnp.concatenate([wide("up"), wide("out")], axis=1)

    for l in reversed(range(LAYERS)):
        if packed[l]:
            plan.add(SCATTERED + l, functools.partial(start_scatter, l))
        for w in ("down",) if packed[l] else ("down", "up", "qkv"):
            key = w + str(l)
            given = functools.partial(take, key)
            name = OUTWARD + number(w, l)
            masks = ways(SCATTER, key)[0]
            plan_scatter(plan, name, given, masks, me, n, functools.partial(final, key))

    plan.run(ORDER if plan.tied else plain_order(plan))

    g_qkv, g_up, g_down = ([results[w + str(l)] for l in range(LAYERS)] for w in WEIGHTS)
    vector_out = g_qkv[0][:, 3 * model_dim :].T

    def pick(at):
        return jnp.stack([vector_out[l * per_layer + at] for l in range(LAYERS)])

    return (
        box["out"],
        box["dx"].astype(f32),
        jnp.stack([pick(0), pick(1)], axis=1),
        jnp.stack([pick(2), pick(3)], axis=1),
        jnp.stack([g[:, : 3 * model_dim] for g in g_qkv]),
        jnp.stack([pick(4), pick(5)], axis=1),
        jnp.stack([g[:, hidden_dim:] for g in g_up]),
        pick(6),
        jnp.stack([g[:, :hidden_dim] for g in g_up]),
        jnp.concatenate([pick(8 + q) for q in range(ratio)], axis=1),
        jnp.stack(g_down),
        pick(7),
    )


GATHER = dict(
    up0=("aybx",),
    down0=("axyb",),
    qkv0=("baxy",),
)
SCATTER = dict(
    up0=("xbay",),
    down0=("yxba",),
    qkv0=("yxba",),
    down1=("byxa",),
)
PLACE = 10
PLACES = {}
ORDER = (
    2011, 0, 200, 400, 2000, 2001, 50, 1, 250, 201, 450, 401, 2050, 2051, 51, 2, 251, 202, 451,
    402, 52, 3, 252, 203, 452, 403, 53, 21, 20, 220, 253, 221, 453, 421, 71, 420, 70, 3000, 270,
    271, 3010, 471, 470, 3020, 3001, 3011, 3031, 1500, 3041, 3051, 2021, 3030, 1400, 3040, 1200,
    1550, 1501, 1450, 1401, 1250, 1201, 3050, 2003, 1000, 3021, 1551, 1502, 1451, 1402, 1251,
    1202, 2053, 1050, 1001, 1552, 1503, 2002, 1452, 1403, 1252, 1203, 1051, 1002, 1553, 1504,
    2052, 1453, 1404, 1253, 1204, 1052, 1003, 1554, 1454, 1254, 1053, 1004, 1054,
)


def solution(mesh):
    n_devices = mesh.shape["dp"] * mesh.shape["seq"]
    rows = P(None, AXES, None)
    last = P(None, None, AXES)
    flat = P(None, AXES)
    batch = P("dp", "seq", None)

    def body(*args):
        return per_device(n_devices, *args)

    return jax.shard_map(
        body,
        mesh=mesh,
        in_specs=(
            batch,
            P("dp", "seq"),
            last,
            last,
            rows,
            last,
            rows,
            flat,
            rows,
            flat,
            rows,
            flat,
            batch,
        ),
        out_specs=(batch, batch, last, last, rows, last, rows, flat, rows, flat, rows, flat),
        check_vma=False,
    )
```

```python
import functools

import jax
import jax.numpy as jnp
from jax import lax
from jax.experimental import pallas as pl
from jax.experimental.pallas import tpu as pltpu
from jax.sharding import PartitionSpec as P

HEAD = 64
BUFFER = 64
LAYERS = 2
AXES = ("dp", "seq")
BLOCKS = 32
SIDE = 128

masked_score = -1e30
f32 = jnp.float32
bf16 = jnp.bfloat16
INV_SQRT2 = 0.7071067811865476
INV_SQRT2PI = 0.3989422804014327

VMEM = pl.BlockSpec(memory_space=pltpu.VMEM)
SMEM = pl.BlockSpec(memory_space=pltpu.SMEM)
ANY = pl.BlockSpec(memory_space=pl.ANY)
weight_now = [10]
VMEM_LIMIT = 58 * 1024 * 1024


def mm(a, b):
    return lax.dot_general(a, b, (((1,), (0,)), ((), ())), preferred_element_type=f32)


def mm_nt(a, b):
    return lax.dot_general(a, b, (((1,), (1,)), ((), ())), preferred_element_type=f32)


def mm_tn(a, b):
    return lax.dot_general(a, b, (((0,), (0,)), ((), ())), preferred_element_type=f32)


def centred(x):
    mean = jnp.mean(x, axis=-1, keepdims=True)
    c = x - mean
    r = lax.rsqrt(jnp.mean(c * c, axis=-1, keepdims=True) + 1e-06)
    return c * r, r


def norm_back(d, n, r, gain):
    e = d * gain
    mean_e = jnp.mean(e, axis=-1, keepdims=True)
    mean_en = jnp.mean(e * n, axis=-1, keepdims=True)
    return r * (e - mean_e - n * mean_en)


def columns_sum(v):
    return jnp.sum(v, axis=0, keepdims=True)


def fetch(colors, parts, me, dst, sem, start=0):
    stop = start + dst.shape[1]
    for first, width, table, at, per, base, fixed in colors:
        low, high = max(start, first), min(stop, first + width)
        if low >= high:
            continue
        rows = dst.shape[0] // len(table)
        for p, offset in enumerate(table):
            owner = p if fixed else me ^ offset
            to_rows = pl.ds(pl.multiple_of(owner * rows, rows), rows)
            cols = pl.ds(low - first, high - low)
            src = parts[at + p // per].at[p % per, pl.ds(base, rows), cols]
            to = dst.at[to_rows, pl.ds(low - start, high - low)]
            pltpu.make_async_copy(src, to, sem).start()


def arrived(dst, sem):
    pltpu.make_async_copy(dst, dst, sem).wait()


def spread(src, out, me, arrays, sem, start):
    first, _, table, at, per, base, fixed = out
    width = src.shape[1]
    rows = src.shape[0] // len(table)
    for p, offset in enumerate(table):
        owner = p if fixed else me ^ offset
        from_rows = pl.ds(pl.multiple_of(owner * rows, rows), rows)
        to = arrays[at + p // per].at[p % per, pl.ds(base, rows), pl.ds(start, width)]
        pltpu.make_async_copy(src.at[from_rows, :], to, sem).start()


def holds(outs, column):
    return [o for o in outs if o[0] <= column < o[0] + o[1]][0]


def attn_fwd_body(colors, many, me_ref, x_ref, flag_ref, gain_ref, shift_ref, bias_ref, *refs):
    parts, refs = refs[:many], refs[many:]
    normed_ref, qkv_ref, att_ref, lse_ref, w, sem = refs
    dim = x_ref.shape[1]
    fetch(colors, parts, me_ref[0], w, sem)
    n, _ = centred(x_ref[...].astype(f32))
    normed_ref[...] = (n * gain_ref[...] + shift_ref[...]).astype(bf16)
    arrived(w, sem)

    def project(c, carry):
        cols = pl.ds(pl.multiple_of(c * 512, 512), 512)
        qkv_ref[:, cols] = (mm(normed_ref[...], w[:, cols]) + bias_ref[:, cols]).astype(bf16)
        return carry

    lax.fori_loop(0, 3 * dim // 512, project, 0)
    allowed = flag_ref[...] > 0
    scale = HEAD ** (-0.5)

    def two_heads(hp, carry):
        base = pl.multiple_of(hp * 128, 128)
        q2 = qkv_ref[:, pl.ds(base, 128)]
        k2 = qkv_ref[:, pl.ds(pl.multiple_of(dim + hp * 128, 128), 128)]
        v2 = qkv_ref[:, pl.ds(pl.multiple_of(2 * dim + hp * 128, 128), 128)]
        outs = []
        for s in range(2):
            cut = slice(s * HEAD, (s + 1) * HEAD)
            score = jnp.where(allowed, mm_nt(k2[:, cut], q2[:, cut]) * scale, masked_score)
            top = jnp.max(score, axis=0, keepdims=True)
            e = jnp.exp(score - top)
            total = jnp.sum(e, axis=0, keepdims=True)
            probs = (e * (1.0 / total)).astype(bf16)
            lse_ref[pl.ds(2 * hp + s, 1), :] = top + jnp.log(total)
            outs.append(mm_tn(probs, v2[:, cut]))
        att_ref[:, pl.ds(base, 128)] = jnp.concatenate(outs, axis=1).astype(bf16)
        return carry

    lax.fori_loop(0, dim // 128, two_heads, 0)


def mlp_up_body(colors, many, me_ref, x_ref, att_ref, ob_ref, gain_ref, shift_ref, ub_ref, *refs):
    parts, refs = refs[:many], refs[many:]
    mid_ref, normed_ref, hidden_ref, slope_ref, w_out, w_up, sem = refs
    ff = ub_ref.shape[1]
    fetch(colors, parts, me_ref[0], w_out, sem.at[0], ff)
    fetch(colors, parts, me_ref[0], w_up, sem.at[1])
    arrived(w_out, sem.at[0])
    mid = x_ref[...].astype(f32) + mm(att_ref[...], w_out[...]) + ob_ref[...]
    mid_ref[...] = mid
    n, _ = centred(mid)
    normed_ref[...] = (n * gain_ref[...] + shift_ref[...]).astype(bf16)
    arrived(w_up, sem.at[1])

    def step(c, carry):
        cols = pl.ds(pl.multiple_of(c * 512, 512), 512)
        u = mm(normed_ref[...], w_up[:, cols]) + ub_ref[:, cols]
        phi = 0.5 + 0.5 * lax.erf(u * INV_SQRT2)
        hidden_ref[:, cols] = (u * phi).astype(bf16)
        slope_ref[:, cols] = phi + u * (INV_SQRT2PI * jnp.exp(-0.5 * u * u))
        return carry

    lax.fori_loop(0, ff // 512, step, 0)


def mlp_down_body(colors, many, last, me_ref, mid_ref, hidden_ref, db_ref, flag_ref, *refs):
    parts, refs = refs[:many], refs[many:]
    out_ref, w, sem = refs
    fetch(colors, parts, me_ref[0], w, sem)
    arrived(w, sem)
    for c in range(0, w.shape[1], 512):
        cols = slice(c, c + 512)
        y = mid_ref[:, cols] + mm(hidden_ref[...], w[:, cols]) + db_ref[:, cols]
        if last:
            y = (y * flag_ref[...]).astype(bf16)
        out_ref[:, cols] = y


def down_grad_body(outs, many, me_ref, grad_ref, hidden_ref, *refs):
    arrays, refs = refs[:many], refs[many:]
    low_ref, sum_ref, perm, tile, sem = refs
    me = me_ref[0]
    grad = grad_ref[...]
    low_ref[...] = grad.astype(bf16)
    sum_ref[...] = columns_sum(grad)
    group = 4
    ((first, width, table, at, per, base, fixed),) = outs
    rows = hidden_ref.shape[1] // len(table)
    for p, offset in enumerate(table):
        owner = pl.ds(pl.multiple_of((p if fixed else me ^ offset) * rows, rows), rows)
        perm[:, p * rows : (p + 1) * rows] = hidden_ref[:, owner]
    pending = [None, None]
    for g in reversed(range(len(table) // group)):
        slot = g % 2
        if pending[slot] is not None:
            pending[slot].wait()
        cut = slice(g * group * rows, (g + 1) * group * rows)
        block = mm_tn(perm[:, cut], low_ref[...])
        tile[slot] = block.astype(bf16).reshape(tile.shape[1:])
        b0 = g * group
        to = arrays[at + b0 // per].at[pl.ds(b0 % per, group), pl.ds(base, rows)]
        pending[slot] = pltpu.make_async_copy(tile.at[slot], to, sem.at[slot])
        pending[slot].start()
    for copy in pending:
        copy.wait()


def mlp_back_body(ups, downs, outs, many, me_ref, grad_ref, low_ref, slope_ref, mid_ref, *refs):
    normed_ref, att_ref, gain_ref, refs = refs[0], refs[1], refs[2], refs[3:]
    many_up, many_down, many_in, many_out = many
    up_parts, refs = refs[:many_up], refs[many_up:]
    down_parts, refs = refs[:many_down], refs[many_down:]
    refs = refs[many_in:]
    halves, refs = refs[:many_out], refs[many_out:]
    d_mid_ref, d_att_ref, g_up_ref, g_gain, g_shift, g_out, refs = (*refs[:6], refs[6:])
    w_down, w_up, w_out, turned, turned_att, d_low_ref, acc, tile, low_mid, sem, out_sem = refs
    me = me_ref[0]
    ff, dim = w_down.shape
    fetch(downs, down_parts, me, w_down, sem.at[0])
    fetch(ups, up_parts, me, w_up, sem.at[1])
    fetch(ups, up_parts, me, w_out, sem.at[2], ff)
    turned[...] = normed_ref[...].T
    turned_att[...] = att_ref[...].T
    acc[...] = jnp.zeros_like(acc)
    arrived(w_down, sem.at[0])

    def first_step(c, carry):
        cols = pl.ds(pl.multiple_of(c * 512, 512), 512)
        d_up = mm_nt(low_ref[...], w_down[cols, :]) * slope_ref[:, cols]
        g_up_ref[:, cols] = columns_sum(d_up)
        d_low_ref[:, cols] = d_up.astype(bf16)
        return carry

    lax.fori_loop(0, ff // 512, first_step, 0)
    arrived(w_up, sem.at[1])

    def flush(slot):
        pltpu.make_async_copy(tile.at[slot], tile.at[slot], out_sem.at[slot]).wait()

    for out in outs:
        first, width = out[:2]
        stop = min(first + width, ff)

        def step(c, carry, out=out, first=first):
            start = pl.multiple_of(c * 512, 512)
            cols = pl.ds(start, 512)
            slot = lax.rem(c, 2)

            @pl.when(c >= 2)
            def _():
                flush(slot)

            tile[slot] = mm(turned[...], d_low_ref[:, cols]).astype(bf16)
            local = pl.multiple_of(start - first, 512)
            spread(tile.at[slot], out, me, halves, out_sem.at[slot], local)
            acc[...] += mm_nt(d_low_ref[:, cols], w_up[:, cols])
            return carry

        lax.fori_loop(first // 512, stop // 512, step, 0)
    n, r = centred(mid_ref[...])
    d = acc[...]
    g_gain[...] = columns_sum(d * n)
    g_shift[...] = columns_sum(d)
    d_mid = grad_ref[...] + norm_back(d, n, r, gain_ref[...])
    d_mid_ref[...] = d_mid
    g_out[...] = columns_sum(d_mid)
    low_mid[...] = d_mid.astype(bf16)
    arrived(w_out, sem.at[2])
    for c in range(dim // 512):
        flush(c % 2)
        tile[c % 2] = mm(turned_att[...], low_mid[:, c * 512 : (c + 1) * 512]).astype(bf16)
        start = ff + c * 512
        out = holds(outs, start)
        spread(tile.at[c % 2], out, me, halves, out_sem.at[c % 2], start - out[0])
    d_att_ref[...] = mm_nt(low_mid[...], w_out[...]).astype(bf16)
    flush(0)
    flush(1)


def attn_back_body(colors, outs, counts, extra, me_ref, d_att_ref, qkv_ref, lse_ref, flag_ref, *refs):
    many, many_in, many_out = counts
    normed_ref, x_ref, d_mid_ref, gain_ref, refs = *refs[:4], refs[4:]
    if extra:
        others_ref, refs = refs[0], refs[1:]
    parts, refs = refs[:many], refs[many:]
    refs = refs[many_in:]
    halves, refs = refs[:many_out], refs[many_out:]
    d_x_ref, g_gain, g_shift, g_query, g_value, refs = (*refs[:5], refs[5:])
    if extra:
        w, d_qkv, turned, tile, sem, out_sem, column, wide = refs
    else:
        w, d_qkv, turned, tile, sem, out_sem = refs
    me = me_ref[0]
    dim = x_ref.shape[1]
    fetch(colors, parts, me, w, sem)
    turned[...] = normed_ref[...].T
    allowed = flag_ref[...] > 0
    scale = HEAD ** (-0.5)

    def two_heads(hp, carry):
        at_q = pl.ds(pl.multiple_of(hp * 128, 128), 128)
        at_k = pl.ds(pl.multiple_of(dim + hp * 128, 128), 128)
        at_v = pl.ds(pl.multiple_of(2 * dim + hp * 128, 128), 128)
        q2, k2, v2, d2 = qkv_ref[:, at_q], qkv_ref[:, at_k], qkv_ref[:, at_v], d_att_ref[:, at_q]
        dq, dk, dv = [], [], []
        for s in range(2):
            cut = slice(s * HEAD, (s + 1) * HEAD)
            q, k, v, d = q2[:, cut], k2[:, cut], v2[:, cut], d2[:, cut]
            score = jnp.where(allowed, mm_nt(k, q) * scale, masked_score)
            probs = jnp.exp(score - lse_ref[pl.ds(2 * hp + s, 1), :])
            dv.append(mm(probs.astype(bf16), d))
            d_probs = mm_nt(v, d)
            inner = jnp.sum(probs * d_probs, axis=0, keepdims=True)
            d_score = (probs * (d_probs - inner)).astype(bf16)
            dq.append(mm_tn(d_score, k) * scale)
            dk.append(mm(d_score, q) * scale)
        d_qkv[:, at_q] = jnp.concatenate(dq, axis=1).astype(bf16)
        d_qkv[:, at_k] = jnp.concatenate(dk, axis=1).astype(bf16)
        d_qkv[:, at_v] = jnp.concatenate(dv, axis=1).astype(bf16)
        return carry

    lax.fori_loop(0, dim // 128, two_heads, 0)

    def flush(slot):
        pltpu.make_async_copy(tile.at[slot], tile.at[slot], out_sem.at[slot]).wait()

    for c in range(3 * dim // 512):
        if c >= 2:
            flush(c % 2)
        tile[c % 2] = mm(turned[...], d_qkv[:, c * 512 : (c + 1) * 512]).astype(bf16)
        out = holds(outs, c * 512)
        spread(tile.at[c % 2], out, me, halves, out_sem.at[c % 2], c * 512 - out[0])
    g_query[...] = columns_sum(d_qkv[:, :dim].astype(f32))
    g_value[...] = columns_sum(d_qkv[:, 2 * dim :].astype(f32))
    arrived(w, sem)
    d = mm_nt(d_qkv[...], w[...])
    n, r = centred(x_ref[...].astype(f32))
    g_gain[...] = columns_sum(d * n)
    g_shift[...] = columns_sum(d)
    d_x_ref[...] = (d_mid_ref[...] + norm_back(d, n, r, gain_ref[...])).astype(d_x_ref.dtype)
    if extra:
        wide[...] = others_ref[...]
        for at, row in zip(extra, (g_gain, g_shift, g_query, g_value)):
            wide[at : at + 1, :] = row[...]
        column[...] = wide[...].T.astype(bf16)
        spread(column, outs[-1], me, halves, sem, 3 * dim - outs[-1][0])
        arrived(column, sem)
    flush(0)
    flush(1)


def shaped(shape, dtype=f32):
    return jax.ShapeDtypeStruct(shape, dtype)


def call(body, name, in_specs, out_shapes, out_specs, scratch, args, aliases=None):
    return pl.pallas_call(
        body,
        in_specs=in_specs,
        out_specs=out_specs,
        out_shape=out_shapes,
        scratch_shapes=scratch,
        input_output_aliases=aliases or {},
        compiler_params=pltpu.CompilerParams(vmem_limit_bytes=VMEM_LIMIT),
        cost_estimate=pl.CostEstimate(
            flops=10 ** weight_now[0], bytes_accessed=0, transcendentals=0
        ),
        name=name,
    )(*args)


def attn_fwd(me, x, flag, gain, shift, bias, weight):
    length, dim = x.shape
    colors, parts = weight
    return call(
        functools.partial(attn_fwd_body, colors, len(parts)),
        "attn_fwd",
        [SMEM] + [VMEM] * 5 + [ANY] * len(parts),
        (
            shaped((length, dim), bf16),
            shaped((length, 3 * dim), bf16),
            shaped((length, dim), bf16),
            shaped((dim // HEAD, length)),
        ),
        (VMEM,) * 4,
        [pltpu.VMEM((dim, 3 * dim), bf16), pltpu.SemaphoreType.DMA],
        (me, x, flag, gain, shift, bias, *parts),
    )


def mlp_up(me, x, att, out_bias, gain, shift, up_bias, weight):
    length, dim = x.shape
    ff = up_bias.shape[1]
    colors, parts = weight
    return call(
        functools.partial(mlp_up_body, colors, len(parts)),
        "mlp_up",
        [SMEM] + [VMEM] * 6 + [ANY] * len(parts),
        (
            shaped((length, dim)),
            shaped((length, dim), bf16),
            shaped((length, ff), bf16),
            shaped((length, ff)),
        ),
        (VMEM,) * 4,
        [
            pltpu.VMEM((dim, dim), bf16),
            pltpu.VMEM((dim, ff), bf16),
            pltpu.SemaphoreType.DMA((2,)),
        ],
        (me, x, att, out_bias, gain, shift, up_bias, *parts),
    )


def mlp_down(me, mid, hidden, down_bias, flag, weight, last):
    length, dim = mid.shape
    ff = hidden.shape[1]
    colors, parts = weight
    return call(
        functools.partial(mlp_down_body, colors, len(parts), last),
        "mlp_down",
        [SMEM] + [VMEM] * 4 + [ANY] * len(parts),
        shaped((length, dim), bf16 if last else f32),
        VMEM,
        [pltpu.VMEM((ff, dim), bf16), pltpu.SemaphoreType.DMA],
        (me, mid, hidden, down_bias, flag, *parts),
    )


def down_grad(me, grad, hidden, outs, shapes):
    length, dim = grad.shape
    ff = hidden.shape[1]
    return call(
        functools.partial(down_grad_body, outs, len(shapes)),
        "down_grad",
        [SMEM, VMEM, VMEM],
        (*shapes, shaped((length, dim), bf16), shaped((1, dim))),
        (ANY,) * len(shapes) + (VMEM, VMEM),
        [
            pltpu.VMEM((length, ff), bf16),
            pltpu.VMEM((2, 4, ff // BLOCKS, dim), bf16),
            pltpu.SemaphoreType.DMA((2,)),
        ],
        (me, grad, hidden),
    )


def mlp_back(me, grad, low, slope, mid, normed, att, gain, up_weight, down_weight, outs, shapes, old):
    length, dim = grad.shape
    ff = slope.shape[1]
    ups, up_parts = up_weight
    downs, down_parts = down_weight
    many = (len(up_parts), len(down_parts), len(old), len(shapes))
    row = shaped((1, dim))
    return call(
        functools.partial(mlp_back_body, ups, downs, outs, many),
        "mlp_back",
        [SMEM] + [VMEM] * 7 + [ANY] * (len(up_parts) + len(down_parts) + len(old)),
        (
            *shapes,
            shaped((length, dim)),
            shaped((length, dim), bf16),
            shaped((1, ff)),
            row,
            row,
            row,
        ),
        (ANY,) * len(shapes) + (VMEM,) * 6,
        [
            pltpu.VMEM((ff, dim), bf16),
            pltpu.VMEM((dim, ff), bf16),
            pltpu.VMEM((dim, dim), bf16),
            pltpu.VMEM((dim, length), bf16),
            pltpu.VMEM((dim, length), bf16),
            pltpu.VMEM((length, ff), bf16),
            pltpu.VMEM((length, dim), f32),
            pltpu.VMEM((2, dim, 512), bf16),
            pltpu.VMEM((length, dim), bf16),
            pltpu.SemaphoreType.DMA((3,)),
            pltpu.SemaphoreType.DMA((2,)),
        ],
        (me, grad, low, slope, mid, normed, att, gain, *up_parts, *down_parts, *old),
        {8 + len(up_parts) + len(down_parts): 0} if old else None,
    )


def attn_back(me, d_att, qkv, lse, flag, normed, x, d_mid, gain, weight, others, at, last, outs, shapes, old):
    length, dim = x.shape
    colors, parts = weight
    extra = () if others is None else tuple(at)
    counts = (len(parts), len(old), len(shapes))
    before = 10 if extra else 9
    row = shaped((1, dim))
    scratch = [
        pltpu.VMEM((dim, 3 * dim), bf16),
        pltpu.VMEM((length, 3 * dim), bf16),
        pltpu.VMEM((dim, length), bf16),
        pltpu.VMEM((2, dim, 512), bf16),
        pltpu.SemaphoreType.DMA,
        pltpu.SemaphoreType.DMA((2,)),
    ]
    if extra:
        scratch += [pltpu.VMEM((dim, SIDE), bf16), pltpu.VMEM((SIDE, dim), f32)]
    return call(
        functools.partial(attn_back_body, colors, outs, counts, extra),
        "attn_back",
        [SMEM] + [VMEM] * (before - 1) + [ANY] * (len(parts) + len(old)),
        (*shapes, shaped((length, dim), bf16 if last else f32), row, row, row, row),
        (ANY,) * len(shapes) + (VMEM,) * 5,
        scratch,
        (me, d_att, qkv, lse, flag, normed, x, d_mid, gain)
        + ((others,) if extra else ())
        + tuple(parts)
        + tuple(old),
        {before + len(parts): 0} if old else None,
    )


def pack_body(a_ref, b_ref, out_ref):
    half = a_ref.shape[0]

    def step(i, carry):
        out_ref[i] = a_ref[i]
        out_ref[half + i] = b_ref[i]
        return carry

    lax.fori_loop(0, half, step, 0)


def pack(a, b):
    shape = (a.shape[0] * 2, *a.shape[1:])
    return call(pack_body, "pack", [VMEM] * 2, shaped(shape, bf16), VMEM, [], (a, b))


def merge_body(keep_ref, got_ref, low_ref, high_ref):
    half = low_ref.shape[0]

    def step(i, carry):
        low_ref[i] = keep_ref[i] + got_ref[i]
        high_ref[i] = keep_ref[half + i] + got_ref[half + i]
        return carry

    lax.fori_loop(0, half, step, 0)


def merge(keep, got):
    half = shaped((keep.shape[0] // 2, *keep.shape[1:]), bf16)
    return call(
        merge_body, "merge", [VMEM] * 2, (half, half), (VMEM, VMEM), [], (keep, got)
    )


def exchange(value, mask, n):
    return lax.ppermute(value, AXES, [(i, i ^ mask) for i in range(n)])


PARTNER = 2
NAMED = dict(x=1, y=4, b=8, a=24)


def other_masks(n):
    bits = n.bit_length() - 1
    return [1 << k for k in range(bits - 1, 1, -1)] + [1]


def span_table(masks):
    table = [0]
    for m in masks:
        table = table + [t ^ m for t in table]
    return tuple(table)


def owners_of(masks, me):
    return me ^ jnp.asarray(span_table(masks), jnp.int32)


def positions_of(masks, me):
    table = span_table(masks)
    inverse = [0] * len(table)
    for p, t in enumerate(table):
        inverse[t] = p
    return jnp.asarray(inverse, jnp.int32)[me ^ jnp.arange(len(table), dtype=jnp.int32)]


class Plan:
    def __init__(self, tied):
        self.actions = {}
        self.tied = tied
        self.last = None

    def ended(self, holder, key):
        self.last = (holder, key)

    def tie(self, value):
        if not self.tied or self.last is None:
            return value
        holder, key = self.last
        value, holder[key] = lax.optimization_barrier((value, holder[key]))
        return value

    def add(self, name, action):
        self.actions[name] = action

    def run(self, order):
        left = dict(self.actions)
        for name in order:
            weight_now[0] = PLACES.get(name, PLACE)
            left.pop(name)()
        assert not left, sorted(left)


def plan_gather(plan, name, own, masks, me, n, ready):
    state = dict(held=own[None])
    last = len(masks) - 1

    def start(k):
        state["got"] = exchange(plan.tie(state["held"]), masks[k], n)

    def finish(k):
        got = plan.tie(state["got"])
        if k < last:
            state["held"] = pack(state["held"], got)
            plan.ended(state, "held")
        else:
            state["end"] = got
            plan.ended(state, "end")

    def cross(k):
        state[k] = exchange(plan.tie(state["held" if k == 1 else "end"]), PARTNER, n)

    def crossed(k):
        state[k] = plan.tie(state[k])
        plan.ended(state, k)
        if k == 2:
            whole = masks + [PARTNER]
            parts = [state["held"], state["end"], state[1], state[2]]
            if n == BLOCKS:
                ready(span_table(whole), parts)
                plan.ended(parts, 3)
            else:
                joined = jnp.concatenate(parts, axis=0)[positions_of(whole, me)]
                joined = joined.reshape(4, BLOCKS // 4, -1, own.shape[1])
                ready(tuple(range(BLOCKS)), list(joined))

    for k in range(len(masks)):
        plan.add(name + k, functools.partial(start, k))
        plan.add(name + k + ENDS, functools.partial(finish, k))
    for k in (1, 2):
        plan.add(name + 19 + k, functools.partial(cross, k))
        plan.add(name + 19 + k + ENDS, functools.partial(crossed, k))


def plan_scatter(plan, name, given, masks, me, n, ready):
    state = {}

    def start(k):
        if k < 0:
            keep, send = given()
            if n != BLOCKS:
                whole = jnp.concatenate([keep, send], axis=0).reshape(n, -1, keep.shape[2])
                whole = whole[owners_of(masks[::-1] + [PARTNER], me)]
                keep, send = whole[: n // 2], whole[n // 2 :]
            state["keep"], state["send"] = keep, send
        mask = PARTNER if k < 0 else masks[k]
        state["got"] = exchange(plan.tie(state["send"]), mask, n)

    def finish(k):
        keep, got = state["keep"], plan.tie(state["got"])
        if k == len(masks) - 1:
            ready((keep.astype(f32) + got.astype(f32))[0])
            return
        state["keep"], state["send"] = merge(keep, got)
        plan.ended(state, "keep")

    for k in range(-1, len(masks)):
        plan.add(name + k + 1, functools.partial(start, k))
        plan.add(name + k + 1 + ENDS, functools.partial(finish, k))


WEIGHTS = ("qkv", "up", "down")
ENDS = 50
OUTWARD = 1000
TOKENS, COTANGENT, OUTPUT, INPUT_GRAD = 2000, 2001, 2002, 2003
GATHERED, SCATTERED = 2010, 2020
KERNELS = 3000


def number(w, l):
    return 100 * (2 * WEIGHTS.index(w) + l)


def plain_order(plan):
    def stage(a):
        if a >= KERNELS:
            return (1, LAYERS * (a - KERNELS >= 30), -(a % 10) if a >= KERNELS + 30 else a % 10, a)
        late = OUTWARD <= a < TOKENS or a % ENDS >= 2 and a >= TOKENS
        return (2 if late else 0, 0, 0, 0)

    return sorted(plan.actions, key=stage)


def per_device(
    n_devices,
    tokens,
    keep,
    norm_gain,
    norm_bias,
    qkv_weight,
    qv_bias,
    out_weight,
    out_bias,
    up_weight,
    up_bias,
    down_weight,
    down_bias,
    cotangent,
):
    n = n_devices
    seq_at = lax.axis_index("seq")
    me = lax.axis_index("dp") * 2 + seq_at
    n_images, local_len, model_dim = tokens.shape
    half_images = n_images // 2
    width = norm_gain.shape[2]
    ratio = up_bias.shape[1] // width
    hidden_dim = up_bias.shape[1] * n
    exact = n == BLOCKS
    who = (me if exact else jnp.zeros_like(me)).reshape(1)
    images = range(half_images)
    plan = Plan(exact and half_images == 1)

    positions = seq_at * local_len + lax.iota(jnp.int32, local_len)
    key_keep = ((keep == 1) | (positions < BUFFER)[None, :]).astype(bf16)

    def halves(value):
        low, high = value[:half_images], value[half_images:]
        mine = jnp.where(seq_at == 0, low, high)
        other = jnp.where(seq_at == 0, high, low)
        return mine, other

    def joined(mine, other):
        return jnp.where(
            seq_at == 0,
            jnp.concatenate([mine, other], axis=0),
            jnp.concatenate([other, mine], axis=0),
        )

    tok_mine, tok_other = halves(tokens)
    cot_mine, cot_other = halves(cotangent)
    keep_mine, keep_other = halves(key_keep)
    box = {}

    def start_tokens():
        below = ((0, 0), (0, 7), (0, model_dim - local_len))
        flags = jnp.pad(keep_other[:, None, :], below)
        sent = jnp.concatenate([tok_other, flags], axis=1)
        box["sent"] = exchange(plan.tie(sent), 1, n)

    def finish_tokens():
        got = plan.tie(box["sent"])
        box["tok"] = jnp.concatenate([tok_mine, got[:, :local_len]], axis=1)
        flags = jnp.concatenate([keep_mine, got[:, local_len, :local_len]], axis=1)
        box["keep"] = flags.astype(f32)[:, :, None]
        plan.ended(box, "tok")

    def start_cotangent():
        box["cot"] = exchange(plan.tie(cot_other), 1, n)

    def finish_cotangent():
        box["cot"] = jnp.concatenate([cot_mine, plan.tie(box["cot"])], axis=1)
        plan.ended(box, "cot")

    plan.add(TOKENS, start_tokens)
    plan.add(TOKENS + ENDS, finish_tokens)
    plan.add(COTANGENT, start_cotangent)
    plan.add(COTANGENT + ENDS, finish_cotangent)

    def columns(l):
        return [norm_gain[l, 0], norm_gain[l, 1], norm_bias[l, 0], norm_bias[l, 1]] + [
            qv_bias[l, 0],
            qv_bias[l, 1],
            out_bias[l],
            down_bias[l],
        ] + [up_bias[l, q * width : (q + 1) * width] for q in range(ratio)]

    stacked = jnp.stack(sum([columns(l) for l in range(LAYERS)], []))
    per_layer = stacked.shape[0] // LAYERS
    stacked = jnp.pad(stacked, ((0, SIDE - stacked.shape[0]), (0, 0))).T

    def ways(table, key):
        return [[NAMED[c] for c in way] for way in table[key]] if exact else [other_masks(n)]

    weights = {}
    packed = [exact and l == LAYERS - 1 for l in range(LAYERS)]
    chunks = dict(qkv=(0, 3), out=(3, 1), up=(4, ratio))
    tall = width * (4 + ratio)

    def receive(key, size, table, parts):
        weights[key] = (((0, size, table, 0, parts[0].shape[0], 0, not exact),), parts)

    def packed_colors(name, start=0):
        at, count = chunks[name]
        same = tuple(range(BLOCKS))
        return tuple(
            (start + c * model_dim, model_dim, same, 0, BLOCKS, width * (at + c), True)
            for c in range(count)
        )

    packed_kinds = dict(
        qkv=packed_colors("qkv"),
        up=packed_colors("up") + packed_colors("out", hidden_dim),
        down=((0, model_dim, tuple(range(BLOCKS)), 0, BLOCKS, tall, True),),
    )

    def start_packed(l):
        def rows(value):
            return value.reshape(width, -1, model_dim).swapaxes(0, 1).reshape(-1, model_dim)

        own = [rows(qkv_weight[l]), out_weight[l], rows(up_weight[l]), down_weight[l]]
        own = plan.tie(jnp.concatenate(own, axis=0))
        whole = lax.all_gather(own, AXES, axis=0, tiled=False)
        for w in WEIGHTS:
            weights[w + str(l)] = (packed_kinds[w], [whole])

    for l in range(LAYERS):
        if packed[l]:
            plan.add(GATHERED + l, functools.partial(start_packed, l))
            continue
        for w in WEIGHTS:
            key = w + str(l)
            if w == "qkv":
                own = qkv_weight[l]
                if l == 0:
                    own = jnp.concatenate([own, stacked], axis=1)
            elif w == "up":
                own = jnp.concatenate([up_weight[l], out_weight[l]], axis=1)
            else:
                own = down_weight[l]
            masks = ways(GATHER, key)[0]
            got = functools.partial(receive, key, own.shape[1])
            plan_gather(plan, number(w, l), own, masks, me, n, got)

    vectors = []

    def read_vectors():
        parts = weights["qkv0"][1]
        side = jnp.concatenate([part[:, :, 3 * model_dim :] for part in parts], axis=0)
        if exact:
            side = side[positions_of(ways(GATHER, "qkv0")[0] + [PARTNER], me)]
        side = side.reshape(model_dim, SIDE).T.astype(f32)
        for l in range(LAYERS):
            rows = side[l * per_layer : (l + 1) * per_layer]
            up_shift = rows[8:].reshape(ratio, n, width).transpose(1, 0, 2).reshape(1, -1)
            no_bias = jnp.zeros((1, model_dim), f32)
            vectors.append(
                dict(
                    gain=(rows[0:1], rows[1:2]),
                    shift=(rows[2:3], rows[3:4]),
                    qkv=jnp.concatenate([rows[4:5], no_bias, rows[5:6]], axis=1),
                    out=rows[6:7],
                    down=rows[7:8],
                    up=up_shift,
                )
            )

    saved = [[None] * LAYERS for _ in images]
    grads = {}
    vector_rows = [[None] * LAYERS for _ in images]
    outs, shapes = {}, {}
    for l in range(LAYERS):
        for w in WEIGHTS:
            key = w + str(l)
            if packed[l] and w != "down":
                outs[key] = packed_kinds[w]
                shapes[key] = [shaped((BLOCKS, tall + width, model_dim), bf16)]
                continue
            total = {"qkv": 3 * model_dim, "up": hidden_dim + model_dim, "down": model_dim}[w]
            total += SIDE if (w, l) == ("qkv", 0) else 0
            masks = ways(SCATTER, key)[0]
            table = span_table(masks[::-1] + [PARTNER]) if exact else tuple(range(BLOCKS))
            rows = (hidden_dim if w == "down" else model_dim) // BLOCKS
            outs[key] = ((0, total, table, 0, BLOCKS // 2, 0, not exact),)
            shapes[key] = [shaped((BLOCKS // 2, rows, total), bf16)] * 2

    def old_of(l, i):
        return [saved[i][l]["packed"]] if packed[l] and "packed" in saved[i][l] else []

    def gave(key, values, l, i):
        if packed[l] and len(values) == 1:
            saved[i][l]["packed"] = values[0]
            return
        grads[key] = values if key not in grads else [a + b for a, b in zip(grads[key], values)]

    def forward_one(l):
        if not vectors:
            read_vectors()
        v = vectors[l]
        for i in images:
            s = saved[i][l] = {}
            s["x"] = box["tok"][i] if l == 0 else saved[i][l - 1]["next"]
            s["normed"], s["qkv"], s["att"], s["lse"] = attn_fwd(
                plan.tie(who),
                s["x"],
                box["keep"][i],
                v["gain"][0],
                v["shift"][0],
                v["qkv"],
                weights["qkv" + str(l)],
            )
            plan.ended(s, "lse")

    def forward_two(l):
        v = vectors[l]
        for i in images:
            s = saved[i][l]
            s["mid"], s["normed_two"], s["hidden"], s["slope"] = mlp_up(
                plan.tie(who),
                s["x"],
                s["att"],
                v["out"],
                v["gain"][1],
                v["shift"][1],
                v["up"],
                weights["up" + str(l)],
            )
            plan.ended(s, "normed_two")

    def forward_three(l):
        for i in images:
            s = saved[i][l]
            s["next"] = mlp_down(
                plan.tie(who),
                s["mid"],
                s["hidden"],
                vectors[l]["down"],
                box["keep"][i],
                weights["down" + str(l)],
                l == LAYERS - 1,
            )
            plan.ended(s, "next")

    def back_one(l):
        for i in images:
            s = saved[i][l]
            if l == LAYERS - 1:
                s["grad"] = box["cot"][i].astype(f32) * box["keep"][i]
            else:
                s["grad"] = saved[i][l + 1]["d_x"]
            key = "down" + str(l)
            *values, s["low"], s["g_down"] = down_grad(
                plan.tie(who), s["grad"], s["hidden"], outs[key], shapes[key]
            )
            plan.ended(s, "low")
            gave(key, values, l, i)

    def back_two(l):
        for i in images:
            s = saved[i][l]
            key = "up" + str(l)
            *values, s["d_mid"], s["d_att"], g_up, g_gain, g_shift, g_out = mlp_back(
                plan.tie(who),
                s["grad"],
                s["low"],
                s["slope"],
                s["mid"],
                s["normed_two"],
                s["att"],
                vectors[l]["gain"][1],
                weights[key],
                weights["down" + str(l)],
                outs[key],
                shapes[key],
                old_of(l, i),
            )
            plan.ended(s, "d_mid")
            gave(key, values, l, i)
            up_rows = g_up.reshape(n, ratio, width).transpose(1, 0, 2).reshape(ratio, -1)
            blank = jnp.zeros_like(g_gain)
            vector_rows[i][l] = [blank, g_gain, blank, g_shift, blank, blank, g_out, s["g_down"]]
            vector_rows[i][l].append(up_rows)

    def back_three(l):
        for i in images:
            s = saved[i][l]
            others = None
            if l == 0:
                others = jnp.concatenate(sum(vector_rows[i], []), axis=0)
                others = jnp.pad(others, ((0, SIDE - others.shape[0]), (0, 0)))
            key = "qkv" + str(l)
            *values, s["d_x"], g_gain, g_shift, g_q, g_v = attn_back(
                plan.tie(who),
                s["d_att"],
                s["qkv"],
                s["lse"],
                box["keep"][i],
                s["normed"],
                s["x"],
                s["d_mid"],
                vectors[l]["gain"][0],
                weights[key],
                others,
                (0, 2, 4, 5),
                l == 0,
                outs[key],
                shapes[key],
                old_of(l, i),
            )
            plan.ended(s, "d_x")
            gave(key, values, l, i)
            rows = vector_rows[i][l]
            rows[0], rows[2], rows[4], rows[5] = g_gain, g_shift, g_q, g_v

    for l in range(LAYERS):
        steps = (forward_one, forward_two, forward_three, back_one, back_two, back_three)
        for at, step in enumerate(steps):
            plan.add(KERNELS + 10 * at + l, functools.partial(step, l))

    def start_back(name, key, l):
        whole = jnp.stack([saved[i][l][key] for i in images])
        box["mine" + name] = whole[:, :local_len]
        box[name] = exchange(plan.tie(whole[:, local_len:]), 1, n)

    def finish_back(name):
        box[name] = joined(box["mine" + name], plan.tie(box[name]))
        plan.ended(box, name)

    plan.add(OUTPUT, functools.partial(start_back, "out", "next", LAYERS - 1))
    plan.add(OUTPUT + ENDS, functools.partial(finish_back, "out"))
    plan.add(INPUT_GRAD, functools.partial(start_back, "dx", "d_x", 0))
    plan.add(INPUT_GRAD + ENDS, functools.partial(finish_back, "dx"))

    results = {}

    def take(key):
        return grads[key]

    def final(key, value):
        results[key] = value
        plan.ended(results, key)

    def start_scatter(l):
        whole = sum(saved[i][l]["packed"] for i in images[1:]) if len(images) > 1 else None
        whole = saved[0][l]["packed"] if whole is None else whole + saved[0][l]["packed"]
        whole = whole.reshape(-1, model_dim)
        got = lax.psum_scatter(whole, AXES, scatter_dimension=0, tiled=True).astype(f32)

        def wide(name):
            at, count = chunks[name]
            part = got[width * at : width * (at + count)]
            return part.reshape(count, width, model_dim).swapaxes(0, 1).reshape(width, -1)

        results["qkv" + str(l)] = wide("qkv")
        results["up" + str(l)] = jnp.concatenate([wide("up"), wide("out")], axis=1)

    for l in reversed(range(LAYERS)):
        if packed[l]:
            plan.add(SCATTERED + l, functools.partial(start_scatter, l))
        for w in ("down",) if packed[l] else ("down", "up", "qkv"):
            key = w + str(l)
            given = functools.partial(take, key)
            name = OUTWARD + number(w, l)
            masks = ways(SCATTER, key)[0]
            plan_scatter(plan, name, given, masks, me, n, functools.partial(final, key))

    plan.run(ORDER if plan.tied else plain_order(plan))

    g_qkv, g_up, g_down = ([results[w + str(l)] for l in range(LAYERS)] for w in WEIGHTS)
    vector_out = g_qkv[0][:, 3 * model_dim :].T

    def pick(at):
        return jnp.stack([vector_out[l * per_layer + at] for l in range(LAYERS)])

    return (
        box["out"],
        box["dx"].astype(f32),
        jnp.stack([pick(0), pick(1)], axis=1),
        jnp.stack([pick(2), pick(3)], axis=1),
        jnp.stack([g[:, : 3 * model_dim] for g in g_qkv]),
        jnp.stack([pick(4), pick(5)], axis=1),
        jnp.stack([g[:, hidden_dim:] for g in g_up]),
        pick(6),
        jnp.stack([g[:, :hidden_dim] for g in g_up]),
        jnp.concatenate([pick(8 + q) for q in range(ratio)], axis=1),
        jnp.stack(g_down),
        pick(7),
    )


GATHER = dict(
    up0=("abyx",),
    down0=("xaby",),
    qkv0=("byxa",),
)
SCATTER = dict(
    up0=("xbay",),
    down0=("yxba",),
    qkv0=("yxba",),
    down1=("byxa",),
)
PLACE = 10
PLACES = {}
ORDER = (
    2011, 0, 200, 400, 2000, 2001, 50, 1, 250, 201, 450, 401, 2050, 2051, 51, 2, 251, 202, 451,
    402, 52, 3, 252, 203, 452, 403, 53, 21, 20, 220, 253, 221, 453, 421, 71, 420, 70, 3000, 270,
    271, 3010, 471, 470, 3020, 3001, 3011, 3031, 1500, 3041, 3051, 2021, 3030, 1400, 3040, 1200,
    1550, 1501, 1450, 1401, 1250, 1201, 3050, 2003, 1000, 1551, 1502, 1451, 1402, 3021, 1251,
    1202, 2053, 1050, 1001, 1552, 1503, 2002, 1452, 1403, 1252, 1203, 1051, 1002, 1553, 1504,
    2052, 1453, 1404, 1253, 1204, 1052, 1003, 1554, 1454, 1254, 1053, 1004, 1054,
)


def solution(mesh):
    n_devices = mesh.shape["dp"] * mesh.shape["seq"]
    rows = P(None, AXES, None)
    last = P(None, None, AXES)
    flat = P(None, AXES)
    batch = P("dp", "seq", None)

    def body(*args):
        return per_device(n_devices, *args)

    return jax.shard_map(
        body,
        mesh=mesh,
        in_specs=(
            batch,
            P("dp", "seq"),
            last,
            last,
            rows,
            last,
            rows,
            flat,
            rows,
            flat,
            rows,
            flat,
            batch,
        ),
        out_specs=(batch, batch, last, last, rows, last, rows, flat, rows, flat, rows, flat),
        check_vma=False,
    )
```
